256 devices in a mesh: tm: 32 (over y, z_hi, core), fiber: 8 (over x, z_lo).
Axes of the slice: x: 4, y: 4, z: 8 (z_hi: 4, z_lo: 2; z = z_hi * 2 + z_lo), core: 2. Of those that a mesh axis runs over, the one named last changes fastest.
Arguments:
- waveform: bfloat16 [4096, 65536], P('fiber', 'tm'), may hold values from -6 to 6
- filters: bfloat16 [512, 256], replicated, may hold values from -0.25 to 0.25
- channel_section: int32 [4096], replicated, may hold values from 0 to 127, never falling along the last dimension, each value on 1 to 64 neighbouring positions
- section_bank: int32 [128, 8], replicated, may hold values from 0 to 1
- conv_bank: bfloat16 [2, 8, 3, 3, 32, 32], P(None, 'fiber'), may hold values from -0.375 to 0.375
Outputs:
- events: bfloat16 [4096, 256, 512], P('tm', 'fiber')
The draws below stay inside these ranges and needn't reach their ends.
Inputs may be any that keep to these rules, and one draw needn't show every extreme that they name: `channel_section`: never falls along the channels; every section has 1 to 64 channels.
All inputs are finite; a program needn't handle non-finite values.
Results may differ from the reference program's by a relative error of at most 0.005.
Values may be sent and summed in bfloat16 or wider, within the bound.
No kernel may reach another device: no remote copies, remote signals or barrier semaphores. Data moves between devices by JAX's collectives and lax.ppermute only.
A program may use at most 128 MiB of HBM per device.

```python
import math
import jax
import jax.numpy as jnp
import numpy as np
from jax import lax

TAPS = 512
HOP = 128
FILTERS = 256
GW = 32
BANKS = 2
SEC_MOST = 64
CHANNELS = 4096
SAMPLES = 65536
FRAMES = 512
GROUPS = 8
SECTIONS = 128


def plant(values, own_key, low, high):
    longest = values.shape.index(max(values.shape))
    spots = []
    for shift in (0, 1):
        where = [jax.random.randint(jax.random.fold_in(own_key, axis), (), 0, length) for axis, length in enumerate(values.shape)]
        where[longest] = (where[longest] + shift) % values.shape[longest]
        spots.append(tuple(where))
    return values.at[spots[0]].set(low).at[spots[1]].set(high)


def block_scale(rng, shape, cuts, least, high):
    def one(position, parts):
        steps = jax.random.uniform(jax.random.fold_in(jax.random.fold_in(rng, 6), position), (parts,), jnp.float32, least / len(cuts), high / len(cuts))
        return jnp.repeat(jnp.exp(steps), shape[position] // parts).reshape((-1,) + (1,) * (len(shape) - position - 1))

    factor_of = one(*cuts[0])
    for cut in cuts[1:]:
        factor_of = factor_of * one(*cut)
    return factor_of


def profile(number_of, total, bound, skew):
    portions = [(1 << 20) // math.isqrt(grade ** skew) + 1 for grade in range(2, number_of + 1)]
    rest, counts = total - bound - (number_of - 1), [1] * (number_of - 1)
    while rest > 0:
        free = [i for i in range(number_of - 1) if counts[i] < bound]
        pool, budget = sum([portions[i] for i in free]), rest
        for i in free:
            extra = min(bound - counts[i], max(1, budget * portions[i] // pool), rest)
            counts[i] = counts[i] + extra
            rest = rest - extra
    return np.array([bound] + counts)


def uneven(rng, amount, total, reach, skew):
    if amount == 2:
        one = jax.random.randint(rng, (), max(1, total - reach), min(reach, total - 1) + 1)
        return jnp.stack([one, total - one])
    lengths = jnp.asarray(profile(amount, total, reach, skew), jnp.int32)
    pairs = (amount - 1) // 2
    giver, taker = lengths[1:1 + 2 * pairs:2], lengths[2:2 + 2 * pairs:2]
    margin = jnp.minimum(giver - 1, reach - taker)
    passed = jax.random.randint(jax.random.fold_in(rng, 1), (pairs,), 0, 1 << 20) % (margin + 1)
    lengths = lengths.at[1:1 + 2 * pairs:2].set(giver - passed).at[2:2 + 2 * pairs:2].set(taker + passed)
    return lengths[jax.random.permutation(jax.random.fold_in(rng, 2), amount)]


def centred(own_key, extent, spread, limit, split=(), kind=jnp.bfloat16):
    values = jax.random.normal(own_key, extent, jnp.float32) * spread
    if len(split) > 0:
        values = block_scale(own_key, extent, split, -0.22, 0.18) * values
    return jnp.clip(values, min=-limit, max=limit).astype(kind)


def setup_inputs(seed: int = 0) -> dict:
    arg_keys = jax.random.split(jax.random.key(seed), 6)
    waveform = centred(arg_keys[0], (CHANNELS, SAMPLES), 1.0, 6.0, ((0, 8), (1, 32)))
    filters = centred(arg_keys[1], (TAPS, FILTERS), TAPS ** -0.5, 0.25)
    channel_section = jnp.searchsorted(jnp.cumsum(uneven(arg_keys[2], SECTIONS, CHANNELS, SEC_MOST, 1)), jnp.arange(CHANNELS), side="right").astype(jnp.int32)
    section_bank = plant(jax.random.randint(arg_keys[3], (SECTIONS, GROUPS), 0, BANKS), jax.random.fold_in(arg_keys[3], 1), 0, BANKS - 1).astype(jnp.int32)
    conv_bank = centred(arg_keys[4], (BANKS, GROUPS, 3, 3, GW, GW), (9 * GW) ** -0.5, 0.375, ((1, 8),))
    return dict(waveform=waveform, filters=filters, channel_section=channel_section, section_bank=section_bank, conv_bank=conv_bank)


def filter_rows(wave_rows, filt):
    count = wave_rows.shape[0]
    blocks = wave_rows.astype(jnp.float32).reshape(count, FRAMES + TAPS // HOP - 1, HOP)
    total = jnp.zeros((count, FRAMES, FILTERS), jnp.float32)
    for k in range(TAPS // HOP):
        total = total + jnp.einsum('cfh,hj->cfj', blocks[:, k:k + FRAMES], filt[k * HOP:(k + 1) * HOP], precision=lax.Precision.HIGHEST)
    return total.astype(jnp.bfloat16)


def reference(waveform, filters, channel_section, section_bank, conv_bank):
    wave = jnp.pad(waveform, ((0, 0), (0, TAPS - HOP)))
    filt = filters.astype(jnp.float32)
    rows = math.gcd(CHANNELS, 64)
    nblock = CHANNELS // rows
    feats = lax.map(lambda i: filter_rows(lax.dynamic_slice_in_dim(wave, i * rows, rows, 0), filt), jnp.arange(nblock, dtype=jnp.int32))
    feats = feats.reshape(CHANNELS, FRAMES, GROUPS, GW).transpose(0, 2, 3, 1)
    padded = jnp.pad(feats, ((1, 1), (0, 0), (0, 0), (1, 1)))
    edge = jnp.array([-1], jnp.int32)
    sec = jnp.concatenate([edge, channel_section.astype(jnp.int32), edge])
    same_lo = (sec[:-2] == sec[1:-1]).astype(jnp.float32)
    same_hi = (sec[2:] == sec[1:-1]).astype(jnp.float32)
    choose = section_bank[channel_section]
    pick_all = (choose[:, :, None] == jnp.arange(BANKS, dtype=jnp.int32)[None, None, :]).astype(jnp.float32)
    weights = conv_bank.astype(jnp.float32)

    def conv_block(i):
        start = (i * rows).astype(jnp.int32)
        xs = lax.dynamic_slice_in_dim(padded, start, rows + 2, 0).astype(jnp.float32)
        low = lax.dynamic_slice_in_dim(same_lo, start, rows, 0)
        high = lax.dynamic_slice_in_dim(same_hi, start, rows, 0)
        pick = lax.dynamic_slice_in_dim(pick_all, start, rows, 0)
        acc = jnp.zeros((rows, GROUPS, BANKS, GW, FRAMES), jnp.float32)
        for d in range(3):
            part = xs[d:d + rows]
            if d == 0:
                part = part * low[:, None, None, None]
            if d == 2:
                part = part * high[:, None, None, None]
            for e in range(3):
                acc = acc + jnp.einsum('bgoi,cgit->cgbot', weights[:, :, d, e], part[..., e:e + FRAMES], precision=lax.Precision.HIGHEST)
        out = jnp.sum(acc * pick[:, :, :, None, None], axis=2)
        return out.astype(jnp.bfloat16).reshape(rows, FILTERS, FRAMES)

    events = lax.map(conv_block, jnp.arange(nblock, dtype=jnp.int32))
    return events.reshape(CHANNELS, FILTERS, FRAMES)
```

```python
import jax
import jax.numpy as jnp
from jax import lax
from jax.experimental import pallas as pl
from jax.experimental.pallas import tpu as pltpu
from jax.sharding import PartitionSpec as P

HOP = 128
GW = 32
AXES = ("tm", "fiber")


def flat(x, y, z, c):
    return ((y * 4 + z // 2) * 2 + c) * 8 + x * 2 + z % 2


def route(move):
    places = [(x, y, z, c) for x in range(4) for y in range(4) for z in range(8) for c in range(2)]
    return [(flat(*p), flat(*move(*p))) for p in places]


def to_block(step, swap):
    def move(x, y, z, c):
        pair, odd = z // 2, z % 2
        late = 0 if pair in (0, 3) else 1
        b = step ^ (pair // 2)
        return ((x - y - (1 if pair == 3 else 0)) % 4, x, 4 * odd + 2 * b + (late ^ odd), c ^ swap)

    return route(move)


def to_earlier(x, y, z, c):
    late = (z % 2) ^ (z // 4)
    return ((x if late else x + 1) % 4, y, z ^ 1, c)


def filter_kernel(where_ref, a_ref, b_ref, c_ref, d_ref, rim_ref, taps_ref, out_ref, seq_ref):
    first, core, keep = where_ref[0], where_ref[1], where_ref[2]
    chans = a_ref.shape[0]
    for step, swap, ref in ((0, 0, a_ref), (0, 1, b_ref), (1, 0, c_ref), (1, 1, d_ref)):
        at = (first ^ step) * 40 + (core ^ swap) * 16
        seq_ref[:, pl.ds(pl.multiple_of(at, 8), 16), :] = ref[...].astype(jnp.float32)
    seq_ref[:, 32:40, :] = seq_ref[:, 40:48, :] * keep.astype(jnp.float32)
    seq_ref[:, 72:75, :] = rim_ref[...].astype(jnp.float32)
    columns = []
    for k in range(4):
        runs = [seq_ref[:, s + k : s + k + 32, :].astype(jnp.bfloat16) for s in (0, 40)]
        columns.append(jnp.concatenate(runs, axis=1).reshape(chans * 64, HOP))
    frames = jnp.concatenate(columns, axis=1)
    feats = lax.dot_general(
        taps_ref[...], frames, (((1,), (1,)), ((), ())), preferred_element_type=jnp.float32
    ).astype(jnp.bfloat16)
    for g in range(8):
        for p in range(chans // 2):
            out_ref[g, p] = feats[g * GW : (g + 1) * GW, p * 128 : (p + 1) * 128]


def conv_kernel(
    slot_ref, recv_ref, low_ref, high_ref, base_ref, row_ref, pick_ref, col_ref, out_ref, x_ref
):
    block = pl.program_id(0)
    lane = lax.broadcasted_iota(jnp.int32, (1, 128), 1)

    def assemble(load, pairs, sides, place):
        v = [load(q).astype(jnp.float32).reshape(pairs * GW, 128) for q in range(8)]
        for e in (-1, 0, 1):
            near = [pltpu.roll(u, 32 - e, 1) for u in v]
            far = [pltpu.roll(u, 96 - e, 1) for u in v]
            for side in sides:
                outer, inner = (near, far) if side else (far, near)
                for m in range(4):
                    t = jnp.where(
                        lane < 32 - e,
                        outer[2 * m],
                        jnp.where(lane < 96 - e, inner[2 * m + 1], outer[(2 * m + 2) % 8]),
                    )
                    if e == -1 and m == 0:
                        t = jnp.where(lane == 0, 0.0, t)
                    if e == 1 and m == 3:
                        t = jnp.where(lane == 127, 0.0, t)
                    t = t.astype(jnp.bfloat16)
                    for p in range(pairs):
                        x_ref[e + 1, place(p, side), :, m * 128 : (m + 1) * 128] = t[
                            p * GW : (p + 1) * GW
                        ]

    def group(g):
        assemble(
            lambda q: recv_ref[slot_ref[q], pl.ds(g * 4, 4)],
            4,
            (0, 1),
            lambda p, side: 8 * g + 1 + 2 * p + side,
        )

    @pl.when(block == 0)
    def _():
        assemble(lambda q: low_ref[slot_ref[8 + q]], 1, (1,), lambda p, side: 0)
        assemble(lambda q: high_ref[slot_ref[16 + q]], 1, (0,), lambda p, side: 129)
        group(0)

    @pl.when(block < pl.num_programs(0) - 1)
    def _():
        group(block + 1)

    w = jnp.where(pick_ref[0] == 1, base_ref[1], base_ref[0])
    w = jnp.where(row_ref[0] == col_ref[0], w, 0.0).astype(jnp.bfloat16)
    x = jnp.concatenate(
        [x_ref[e, pl.ds(8 * block, 10)].reshape(10 * GW, 512) for e in range(3)], axis=0
    )
    res = jnp.dot(w, x, preferred_element_type=jnp.float32)
    out_ref[...] = res.astype(jnp.bfloat16).reshape(8, GW, 512)


def shards(waveform, filters, channel_section, section_bank, conv_bank):
    tm, fiber = lax.axis_index("tm"), lax.axis_index("fiber")
    y, zh, core, x, z0 = tm // 8, (tm // 2) % 4, tm % 2, fiber // 2, fiber % 2
    z2, z1 = zh // 2, zh % 2
    late = z0 ^ z2
    first = 1 ^ z1 ^ late
    keep = jnp.where((late == 0) & ((y - x) % 4 == 0), 0, 1)
    where = jnp.stack([first, core, keep]).astype(jnp.int32)

    wave = waveform.reshape(4, 128, 16, HOP)
    got = []
    for step in (0, 1):
        for swap in (0, 1):
            part = lax.dynamic_index_in_dim(wave, 2 * (step ^ z2) + (core ^ swap), 0, False)
            got.append(lax.ppermute(part, AXES, to_block(step, swap)))
    head = [g[:, :3] for g in got]
    head = jnp.where(
        first == 0,
        jnp.where(core == 0, head[0], head[1]),
        jnp.where(core == 0, head[2], head[3]),
    )
    rim = lax.ppermute(head, AXES, route(to_earlier))

    piece = pl.BlockSpec((16, 16, HOP), lambda i, s: (i, 0, 0))
    feats = pl.pallas_call(
        filter_kernel,
        out_shape=jax.ShapeDtypeStruct((8, 64, GW, 128), jnp.bfloat16),
        grid_spec=pltpu.PrefetchScalarGridSpec(
            num_scalar_prefetch=1,
            grid=(8,),
            in_specs=[piece] * 4
            + [
                pl.BlockSpec((16, 3, HOP), lambda i, s: (i, 0, 0)),
                pl.BlockSpec((256, 512), lambda i, s: (0, 0)),
            ],
            out_specs=pl.BlockSpec((8, 8, GW, 128), lambda i, s: (0, i, 0, 0)),
            scratch_shapes=[pltpu.VMEM((16, 80, HOP), jnp.float32)],
        ),
        cost_estimate=pl.CostEstimate(
            flops=2 * 8192 * 512 * 256, bytes_accessed=6 << 20, transcendentals=0
        ),
        name="filterbank",
    )(where, *got, rim, filters.T)

    recv = lax.all_to_all(feats, "fiber", 0, 0, tiled=True)
    up = [(i, i + 1) for i in range(31)]
    low = lax.ppermute(recv[:, 63:], "tm", up)
    high = lax.ppermute(recv[:, :1], "tm", [(j, i) for i, j in up])

    def slots(t):
        q = jnp.arange(8, dtype=jnp.int32)
        return 2 * ((t // 8 - q // 2) % 4) + ((q % 2) ^ ((t // 4) % 2))

    slot = jnp.concatenate(
        [slots(tm), slots(jnp.maximum(tm - 1, 0)), slots(jnp.minimum(tm + 1, 31))]
    ).astype(jnp.int32)

    edge = jnp.array([-1], jnp.int32)
    sec = lax.dynamic_slice_in_dim(
        jnp.concatenate([edge, channel_section, edge]), tm * 128, 130, 0
    )
    middle = sec[1:-1]
    table = lax.dynamic_slice_in_dim(section_bank, fiber, 1, 1)
    onehot = (middle[:, None] == jnp.arange(table.shape[0], dtype=jnp.int32)[None, :]).astype(
        jnp.int32
    )
    choose = jnp.sum(onehot * table[:, 0][None, :], axis=1)
    rows = jnp.repeat(middle, GW).reshape(16, 256, 1)
    pick = jnp.repeat(choose, GW).reshape(16, 256, 1)
    cols = jnp.stack([sec[8 * b : 8 * b + 10] for b in range(16)])
    cols = jnp.tile(jnp.repeat(cols, GW, axis=1), (1, 3)).reshape(16, 1, 960)
    spread = (
        jnp.arange(10)[None, :, None]
        == jnp.arange(8)[:, None, None] + jnp.arange(3)[None, None, :]
    ).astype(jnp.bfloat16)
    base = jnp.einsum(
        "bdeoi,cxd->bcoexi", conv_bank[:, 0], spread, preferred_element_type=jnp.float32
    ).reshape(2, 256, 960)

    whole = lambda *shape: pl.BlockSpec(shape, lambda i, s: (0,) * len(shape))
    return pl.pallas_call(
        conv_kernel,
        out_shape=jax.ShapeDtypeStruct((128, GW, 512), jnp.bfloat16),
        grid_spec=pltpu.PrefetchScalarGridSpec(
            num_scalar_prefetch=1,
            grid=(16,),
            in_specs=[
                whole(8, 64, GW, 128),
                whole(8, 1, GW, 128),
                whole(8, 1, GW, 128),
                whole(2, 256, 960),
                pl.BlockSpec((1, 256, 1), lambda i, s: (i, 0, 0)),
                pl.BlockSpec((1, 256, 1), lambda i, s: (i, 0, 0)),
                pl.BlockSpec((1, 1, 960), lambda i, s: (i, 0, 0)),
            ],
            out_specs=pl.BlockSpec((8, GW, 512), lambda i, s: (i, 0, 0)),
            scratch_shapes=[pltpu.VMEM((3, 130, GW, 512), jnp.bfloat16)],
        ),
        cost_estimate=pl.CostEstimate(
            flops=2 * 4096 * 960 * 512, bytes_accessed=8 << 20, transcendentals=0
        ),
        name="sectionconv",
    )(slot, recv, low, high, base, rows, pick, cols)


def solution(mesh):
    placed = (P("fiber", "tm"), P(), P(), P(), P(None, "fiber", None, None, None, None))
    return jax.shard_map(
        shards, mesh=mesh, in_specs=placed, out_specs=P("tm", "fiber", None), check_vma=False
    )
```

```python
import jax
import jax.numpy as jnp
from jax import lax
from jax.experimental import pallas as pl
from jax.experimental.pallas import tpu as pltpu
from jax.sharding import PartitionSpec as P

HOP = 128
GW = 32
AXES = ("tm", "fiber")


PLACES = [(x, y, z, c) for x in range(4) for y in range(4) for z in range(8) for c in range(2)]


def flat(x, y, z, c):
    return ((y * 4 + z // 2) * 2 + c) * 8 + x * 2 + z % 2


def spot(x, y, late, odd, b, core, early):
    nx = (x - y + 2 * b + core - early) % 4
    return flat(nx, x, 4 * odd + 2 * b + (late ^ odd), core)


def bulk_route(step, swap):
    pairs = []
    for x, y, z, c in PLACES:
        pair, odd = z // 2, z % 2
        late = 0 if pair in (0, 3) else 1
        b = step ^ (pair // 2)
        pairs.append((flat(x, y, z, c), spot(x, y, late, odd, b, c ^ swap, int(pair == 3))))
    return pairs


def rim_route(b, core):
    return [
        (flat(x, y, z, c), spot(x, y, int(z // 2 == 3), z % 2, b, core, 0))
        for x, y, z, c in PLACES
        if c == 0 and z // 2 in (1, 3)
    ]


def filter_kernel(where_ref, *refs):
    pieces, rims, (taps_ref, out_ref, seq_ref) = refs[:4], refs[4:8], refs[8:]
    first, core, keep = where_ref[0], where_ref[1], where_ref[2]
    chans = seq_ref.shape[0]

    @pl.loop(0, pieces[0].shape[0] // chans)
    def _(i):
        rows = pl.ds(i * chans, chans)
        for j, ref in enumerate(pieces):
            at = (first ^ (j >> 1)) * 48 + (core ^ (j & 1)) * 16
            seq_ref[:, pl.ds(pl.multiple_of(at, 16), 16), :] = ref[rows]
        seq_ref[:, 32:48, :] = seq_ref[:, 48:64, :] * keep.astype(jnp.bfloat16)
        seq_ref[:, 80:83, :] = (rims[0][rows] + rims[1][rows]) + (rims[2][rows] + rims[3][rows])
        columns = []
        for k in range(4):
            runs = [seq_ref[:, s + k : s + k + 32, :] for s in (0, 48)]
            columns.append(jnp.concatenate(runs, axis=1).reshape(chans * 64, HOP))
        frames = jnp.concatenate(columns, axis=1)
        feats = lax.dot_general(
            taps_ref[...], frames, (((1,), (1,)), ((), ())), preferred_element_type=jnp.float32
        ).astype(jnp.bfloat16)
        for g in range(8):
            for p in range(chans // 2):
                out_ref[g, i * (chans // 2) + p] = feats[
                    g * GW : (g + 1) * GW, p * 128 : (p + 1) * 128
                ]


def weight_kernel(flag_ref, kern_ref, out_ref, base_ref):
    block = pl.program_id(0)

    @pl.when(block == 0)
    def _():
        r = lax.broadcasted_iota(jnp.int32, (288, 960), 0)
        k = lax.broadcasted_iota(jnp.int32, (288, 960), 1)
        lag = k - r - 224 * ((r >= 96).astype(jnp.int32) + (r >= 192).astype(jnp.int32))
        for c in range(8):
            spread = jnp.where(lag == 32 * c, 1.0, 0.0).astype(jnp.bfloat16)
            base_ref[c] = jnp.dot(kern_ref[...], spread, preferred_element_type=jnp.float32)

    k = lax.broadcasted_iota(jnp.int32, (1, 960), 1)
    k = k - 320 * ((k >= 320).astype(jnp.int32) + (k >= 640).astype(jnp.int32))
    for c in range(8):
        at = block * 8 + c
        low, high = flag_ref[1, at].astype(jnp.float32), flag_ref[2, at].astype(jnp.float32)
        mask = jnp.where(k < 32 * c + 32, low, jnp.where(k >= 32 * c + 64, high, 1.0))
        rows = base_ref[c, pl.ds(pl.multiple_of(flag_ref[0, at] * GW, GW), GW), :]
        out_ref[0, c * GW : (c + 1) * GW, :] = (rows * mask).astype(jnp.bfloat16)


def assemble(x_ref, load, pairs, sides, place):
    size = pairs * GW
    lane = lax.broadcasted_iota(jnp.int16, (size, 128), 1)
    v = [load(q).reshape(size, 128) for q in range(8)]
    near = [pltpu.roll(u, 32, 1) for u in v]
    far = [pltpu.roll(u, 96, 1) for u in v]
    zero = jnp.zeros((size, 128), jnp.bfloat16)
    for side in sides:
        outer, inner = (near, far) if side else (far, near)
        t = [
            jnp.where(
                lane < 32,
                outer[2 * m],
                jnp.where(lane < 96, inner[2 * m + 1], outer[(2 * m + 2) % 8]),
            )
            for m in range(4)
        ]
        back = [pltpu.roll(u, 1, 1) for u in t]
        ahead = [pltpu.roll(u, 127, 1) for u in t]
        for m in range(4):
            before = jnp.where(lane == 0, back[m - 1] if m else zero, back[m])
            after = jnp.where(lane == 127, ahead[m + 1] if m < 3 else zero, ahead[m])
            for e, u in enumerate((before, t[m], after)):
                for p in range(pairs):
                    x_ref[e, place(p, side), :, m * 128 : (m + 1) * 128] = u[
                        p * GW : (p + 1) * GW
                    ]


def conv_kernel(slot_ref, recv_ref, w_ref, out_ref, x_ref):
    step = pl.program_id(0)

    def group(g):
        assemble(
            x_ref,
            lambda q: recv_ref[slot_ref[q], pl.ds(g * 4, 4)],
            4,
            (0, 1),
            lambda p, side: 8 * g + 1 + 2 * p + side,
        )

    def multiply():
        x = jnp.concatenate(
            [x_ref[e, pl.ds(8 * step, 10)].reshape(10 * GW, 512) for e in range(3)], axis=0
        )
        res = jnp.dot(w_ref[0], x, preferred_element_type=jnp.float32)
        out_ref[...] = res.astype(jnp.bfloat16).reshape(8, GW, 512)

    @pl.when(step == 0)
    def _():
        assemble(x_ref, lambda q: recv_ref[slot_ref[q], 64], 1, (0, 1), lambda p, side: 129 * side)
        group(0)

    @pl.when(step < 15)
    def _():
        group(step + 1)
        multiply()

    @pl.when(step == 15)
    def _():
        multiply()


def whole(*shape):
    return pl.BlockSpec(shape, lambda i, s: (0,) * len(shape))


def shards(waveform, filters, channel_section, section_bank, conv_bank):
    tm, fiber = lax.axis_index("tm"), lax.axis_index("fiber")
    y, zh, core, x, z0 = tm >> 3, (tm >> 1) & 3, tm & 1, fiber >> 1, fiber & 1
    z2, z1 = zh >> 1, zh & 1
    late = z0 ^ z2
    first = 1 ^ z1 ^ late
    turn = 2 * z1 + core
    vmem = pl.BlockSpec(memory_space=pltpu.VMEM)

    up = [(i, i + 1) for i in range(7)]
    row_low = lax.ppermute(waveform[511:], "fiber", up)
    row_high = lax.ppermute(waveform[:1], "fiber", [(j, i) for i, j in up])
    edge_rows = jnp.concatenate(
        [row_low]
        + [waveform[i : i + 1] for i in (128, 127, 256, 255, 384, 383)]
        + [row_high],
        axis=0,
    ).reshape(4, 2, 2048)

    def block_rows(at):
        main = lax.dynamic_slice_in_dim(waveform, 128 * at, 128, 0)
        sides = lax.dynamic_index_in_dim(edge_rows, at, 0, False)
        return main.reshape(128, 16, HOP), sides.reshape(2, 16, HOP)

    pieces, rims = [], []
    for step in (0, 1):
        for swap in (0, 1):
            part = jnp.concatenate(block_rows(2 * (step ^ z2) + (core ^ swap)), axis=0)
            pieces.append(lax.ppermute(part, AXES, bulk_route(step, swap)))
    for b in (0, 1):
        for c in (0, 1):
            part = jnp.concatenate(
                [
                    waveform[128 * (2 * b + c) : 128 * (2 * b + c + 1), : 3 * HOP],
                    edge_rows[2 * b + c, :, : 3 * HOP],
                ],
                axis=0,
            ).reshape(130, 3, HOP)
            rims.append(lax.ppermute(part, AXES, rim_route(b, c)))

    edge = jnp.array([-1], jnp.int32)
    sec = lax.dynamic_slice_in_dim(
        jnp.concatenate([edge, channel_section, edge]), tm * 128, 130, 0
    )
    middle = sec[1:-1]
    table = lax.dynamic_slice_in_dim(section_bank, fiber, 1, 1)
    onehot = (middle[:, None] == jnp.arange(table.shape[0], dtype=jnp.int32)[None, :]).astype(
        jnp.int32
    )
    choose = jnp.sum(onehot * table[:, 0][None, :], axis=1)
    flags = jnp.stack([choose, sec[:-2] == middle, sec[2:] == middle]).astype(jnp.int32)
    kern = conv_bank[:, 0].transpose(0, 3, 2, 1, 4).reshape(64, 288)
    weights = pl.pallas_call(
        weight_kernel,
        out_shape=jax.ShapeDtypeStruct((16, 256, 960), jnp.bfloat16),
        grid_spec=pltpu.PrefetchScalarGridSpec(
            num_scalar_prefetch=1,
            grid=(16,),
            in_specs=[whole(64, 288)],
            out_specs=pl.BlockSpec((1, 256, 960), lambda i, s: (i, 0, 0)),
            scratch_shapes=[pltpu.VMEM((8, 64, 960), jnp.float32)],
        ),
        cost_estimate=pl.CostEstimate(
            flops=8 * 2 * 64 * 288 * 960, bytes_accessed=8 << 20, transcendentals=0
        ),
        name="weights",
    )(flags, kern)

    keep = jnp.where((late == 0) & (((y - x + turn) & 3) == 0), 0, 1)
    where = jnp.stack([first, core, keep]).astype(jnp.int32)
    feats = pl.pallas_call(
        filter_kernel,
        out_shape=jax.ShapeDtypeStruct((8, 65, GW, 128), jnp.bfloat16),
        in_specs=[pl.BlockSpec(memory_space=pltpu.SMEM)] + [vmem] * 9,
        out_specs=vmem,
        scratch_shapes=[pltpu.VMEM((26, 96, HOP), jnp.bfloat16)],
        cost_estimate=pl.CostEstimate(
            flops=2 * 8320 * 512 * 256, bytes_accessed=6 << 20, transcendentals=0
        ),
        name="filterbank",
    )(where, *pieces, *rims, filters.T)
    recv = lax.all_to_all(feats, "fiber", 0, 0, tiled=True)

    q = jnp.arange(8, dtype=jnp.int32)
    slot = (2 * ((y + turn - (q >> 1)) & 3) + ((q & 1) ^ z2)).astype(jnp.int32)
    return pl.pallas_call(
        conv_kernel,
        out_shape=jax.ShapeDtypeStruct((128, GW, 512), jnp.bfloat16),
        grid_spec=pltpu.PrefetchScalarGridSpec(
            num_scalar_prefetch=1,
            grid=(16,),
            in_specs=[vmem, pl.BlockSpec((1, 256, 960), lambda i, s: (i, 0, 0))],
            out_specs=pl.BlockSpec((8, GW, 512), lambda i, s: (i, 0, 0)),
            scratch_shapes=[pltpu.VMEM((3, 130, GW, 512), jnp.bfloat16)],
        ),
        cost_estimate=pl.CostEstimate(
            flops=16 * 2 * 256 * 960 * 512, bytes_accessed=16 << 20, transcendentals=0
        ),
        name="conv",
    )(slot, recv, weights)


def solution(mesh):
    placed = (P("fiber", "tm"), P(), P(), P(), P(None, "fiber", None, None, None, None))

    return jax.shard_map(
        shards, mesh=mesh, in_specs=placed, out_specs=P("tm", "fiber", None), check_vma=False
    )
```

```python
import jax
import jax.numpy as jnp
from jax import lax
from jax.experimental import pallas as pl
from jax.experimental.pallas import tpu as pltpu
from jax.sharding import PartitionSpec as P

HOP = 128
GW = 32
AXES = ("tm", "fiber")


PLACES = [(x, y, z, c) for x in range(4) for y in range(4) for z in range(8) for c in range(2)]


def flat(x, y, z, c):
    return ((y * 4 + z // 2) * 2 + c) * 8 + x * 2 + z % 2


def spot(x, y, late, odd, b, core, early):
    nx = (x - y + 2 * b + core - early) % 4
    return flat(nx, x, 4 * odd + 2 * b + (late ^ odd), core)


def bulk_route(step, swap):
    pairs = []
    for x, y, z, c in PLACES:
        pair, odd = z // 2, z % 2
        late = 0 if pair in (0, 3) else 1
        b = step ^ (pair // 2)
        pairs.append((flat(x, y, z, c), spot(x, y, late, odd, b, c ^ swap, int(pair == 3))))
    return pairs


def rim_route(b, core):
    return [
        (flat(x, y, z, c), spot(x, y, int(z // 2 == 3), z % 2, b, core, 0))
        for x, y, z, c in PLACES
        if c == 0 and z // 2 in (1, 3)
    ]


def filter_kernel(where_ref, *refs):
    pieces, edges, rims, (taps_ref, out_ref, seq_ref) = refs[:4], refs[4:8], refs[8:12], refs[12:]
    first, core, keep = where_ref[0], where_ref[1], where_ref[2]

    def filtered(parts, rows, chans, place):
        for j, ref in enumerate(parts):
            at = (first ^ (j >> 1)) * 48 + (core ^ (j & 1)) * 16
            seq_ref[:chans, pl.ds(pl.multiple_of(at, 16), 16), :] = ref[rows]
        seq_ref[:chans, 32:48, :] = seq_ref[:chans, 48:64, :] * keep.astype(jnp.bfloat16)
        rim = (rims[0][place] + rims[1][place]) + (rims[2][place] + rims[3][place])
        seq_ref[:chans, 80:83, :] = rim
        columns = []
        for k in range(4):
            runs = [seq_ref[:chans, s + k : s + k + 32, :] for s in (0, 48)]
            columns.append(jnp.concatenate(runs, axis=1).reshape(chans * 64, HOP))
        frames = jnp.concatenate(columns, axis=1)
        return lax.dot_general(
            taps_ref[...], frames, (((1,), (1,)), ((), ())), preferred_element_type=jnp.float32
        ).astype(jnp.bfloat16)

    @pl.loop(0, 8)
    def _(i):
        feats = filtered(pieces, pl.ds(i * 16, 16), 16, pl.ds(i * 16, 16))
        for g in range(8):
            for p in range(8):
                out_ref[g, i * 8 + p] = feats[g * GW : (g + 1) * GW, p * 128 : (p + 1) * 128]

    feats = filtered(edges, slice(0, 2), 2, slice(128, 130))
    for g in range(8):
        out_ref[g, 64] = feats[g * GW : (g + 1) * GW, :]


def weight_kernel(flag_ref, kern_ref, out_ref, base_ref):
    block = pl.program_id(0)

    @pl.when(block == 0)
    def _():
        r = lax.broadcasted_iota(jnp.int32, (288, 960), 0)
        k = lax.broadcasted_iota(jnp.int32, (288, 960), 1)
        lag = k - r - 224 * ((r >= 96).astype(jnp.int32) + (r >= 192).astype(jnp.int32))
        for c in range(8):
            spread = jnp.where(lag == 32 * c, 1.0, 0.0).astype(jnp.bfloat16)
            base_ref[c] = jnp.dot(kern_ref[...], spread, preferred_element_type=jnp.float32)

    k = lax.broadcasted_iota(jnp.int32, (1, 960), 1)
    k = k - 320 * ((k >= 320).astype(jnp.int32) + (k >= 640).astype(jnp.int32))
    for c in range(8):
        at = block * 8 + c
        low, high = flag_ref[1, at].astype(jnp.float32), flag_ref[2, at].astype(jnp.float32)
        mask = jnp.where(k < 32 * c + 32, low, jnp.where(k >= 32 * c + 64, high, 1.0))
        rows = base_ref[c, pl.ds(pl.multiple_of(flag_ref[0, at] * GW, GW), GW), :]
        out_ref[0, c * GW : (c + 1) * GW, :] = (rows * mask).astype(jnp.bfloat16)


def assemble(x_ref, load, pairs, sides, place):
    size = pairs * GW
    lane = lax.broadcasted_iota(jnp.int16, (size, 128), 1)
    v = [load(q).reshape(size, 128) for q in range(8)]
    near = [pltpu.roll(u, 32, 1) for u in v]
    far = [pltpu.roll(u, 96, 1) for u in v]
    zero = jnp.zeros((size, 128), jnp.bfloat16)
    for side in sides:
        outer, inner = (near, far) if side else (far, near)
        t = [
            jnp.where(
                lane < 32,
                outer[2 * m],
                jnp.where(lane < 96, inner[2 * m + 1], outer[(2 * m + 2) % 8]),
            )
            for m in range(4)
        ]
        back = [pltpu.roll(u, 1, 1) for u in t]
        ahead = [pltpu.roll(u, 127, 1) for u in t]
        for m in range(4):
            before = jnp.where(lane == 0, back[m - 1] if m else zero, back[m])
            after = jnp.where(lane == 127, ahead[m + 1] if m < 3 else zero, ahead[m])
            for e, u in enumerate((before, t[m], after)):
                for p in range(pairs):
                    x_ref[e, place(p, side), :, m * 128 : (m + 1) * 128] = u[
                        p * GW : (p + 1) * GW
                    ]


def conv_kernel(slot_ref, recv_ref, w_ref, out_ref, x_ref):
    step = pl.program_id(0)

    def group(g):
        assemble(
            x_ref,
            lambda q: recv_ref[slot_ref[q], pl.ds(g * 4, 4)],
            4,
            (0, 1),
            lambda p, side: 8 * g + 1 + 2 * p + side,
        )

    def multiply():
        x = jnp.concatenate(
            [x_ref[e, pl.ds(8 * step, 10)].reshape(10 * GW, 512) for e in range(3)], axis=0
        )
        res = jnp.dot(w_ref[0], x, preferred_element_type=jnp.float32)
        out_ref[...] = res.astype(jnp.bfloat16).reshape(8, GW, 512)

    @pl.when(step == 0)
    def _():
        assemble(x_ref, lambda q: recv_ref[slot_ref[q], 64], 1, (0, 1), lambda p, side: 129 * side)
        group(0)

    @pl.when(step < 15)
    def _():
        group(step + 1)
        multiply()

    @pl.when(step == 15)
    def _():
        multiply()


def whole(*shape):
    return pl.BlockSpec(shape, lambda i, s: (0,) * len(shape))


def shards(waveform, filters, channel_section, section_bank, conv_bank):
    tm, fiber = lax.axis_index("tm"), lax.axis_index("fiber")
    y, zh, core, x, z0 = tm >> 3, (tm >> 1) & 3, tm & 1, fiber >> 1, fiber & 1
    z2, z1 = zh >> 1, zh & 1
    late = z0 ^ z2
    first = 1 ^ z1 ^ late
    turn = 2 * z1 + core
    vmem = pl.BlockSpec(memory_space=pltpu.VMEM)

    def send(part, perm, axes=AXES):
        return lax.ppermute(part, axes, perm)

    steps = [(s, w) for s in (0, 1) for w in (0, 1)]
    place = {(s, w): 2 * (s ^ z2) + (core ^ w) for s, w in steps}

    def bulk(wave, s, w):
        part = lax.dynamic_slice_in_dim(wave, 128 * place[s, w], 128, 0).reshape(128, 16, HOP)
        return send(part, bulk_route(s, w))

    pieces = [bulk(waveform, 0, 0), bulk(waveform, 0, 1)]
    up = [(i, i + 1) for i in range(7)]
    row_low = send(waveform[511:], up, "fiber")
    row_high = send(waveform[:1], [(j, i) for i, j in up], "fiber")
    wave, row_low, row_high = lax.optimization_barrier((waveform, row_low, row_high))
    rows = jnp.concatenate(
        [row_low] + [wave[i : i + 1] for i in (128, 127, 256, 255, 384, 383)] + [row_high], axis=0
    ).reshape(4, 2, 2048)
    rims = []
    for b, c in steps:
        at = 2 * b + c
        part = jnp.concatenate(
            [wave[128 * at : 128 * (at + 1), : 3 * HOP], rows[at, :, : 3 * HOP]], axis=0
        ).reshape(130, 3, HOP)
        rims.append(send(part, rim_route(b, c)))
    pieces += [bulk(wave, 1, 0), bulk(wave, 1, 1)]
    edges = [
        send(
            lax.dynamic_index_in_dim(rows, place[s, w], 0, False).reshape(2, 16, HOP),
            bulk_route(s, w),
        )
        for s, w in steps
    ]

    edge = jnp.array([-1], jnp.int32)
    sec = lax.dynamic_slice_in_dim(
        jnp.concatenate([edge, channel_section, edge]), tm * 128, 130, 0
    )
    middle = sec[1:-1]
    table = lax.dynamic_slice_in_dim(section_bank, fiber, 1, 1)
    onehot = (middle[:, None] == jnp.arange(table.shape[0], dtype=jnp.int32)[None, :]).astype(
        jnp.int32
    )
    choose = jnp.sum(onehot * table[:, 0][None, :], axis=1)
    flags = jnp.stack([choose, sec[:-2] == middle, sec[2:] == middle]).astype(jnp.int32)
    kern = conv_bank[:, 0].transpose(0, 3, 2, 1, 4).reshape(64, 288)
    weights = pl.pallas_call(
        weight_kernel,
        out_shape=jax.ShapeDtypeStruct((16, 256, 960), jnp.bfloat16),
        grid_spec=pltpu.PrefetchScalarGridSpec(
            num_scalar_prefetch=1,
            grid=(16,),
            in_specs=[whole(64, 288)],
            out_specs=pl.BlockSpec((1, 256, 960), lambda i, s: (i, 0, 0)),
            scratch_shapes=[pltpu.VMEM((8, 64, 960), jnp.float32)],
        ),
        cost_estimate=pl.CostEstimate(
            flops=8 * 2 * 64 * 288 * 960, bytes_accessed=8 << 20, transcendentals=0
        ),
        name="weights",
    )(flags, kern)

    keep = jnp.where((late == 0) & (((y - x + turn) & 3) == 0), 0, 1)
    where = jnp.stack([first, core, keep]).astype(jnp.int32)
    feats = pl.pallas_call(
        filter_kernel,
        out_shape=jax.ShapeDtypeStruct((8, 65, GW, 128), jnp.bfloat16),
        in_specs=[pl.BlockSpec(memory_space=pltpu.SMEM)] + [vmem] * 13,
        out_specs=vmem,
        scratch_shapes=[pltpu.VMEM((16, 96, HOP), jnp.bfloat16)],
        cost_estimate=pl.CostEstimate(
            flops=2 * 8320 * 512 * 256, bytes_accessed=6 << 20, transcendentals=0
        ),
        name="filterbank",
    )(where, *pieces, *edges, *rims, filters.T)
    recv = lax.all_to_all(feats, "fiber", 0, 0, tiled=True)

    q = jnp.arange(8, dtype=jnp.int32)
    slot = (2 * ((y + turn - (q >> 1)) & 3) + ((q & 1) ^ z2)).astype(jnp.int32)
    return pl.pallas_call(
        conv_kernel,
        out_shape=jax.ShapeDtypeStruct((128, GW, 512), jnp.bfloat16),
        grid_spec=pltpu.PrefetchScalarGridSpec(
            num_scalar_prefetch=1,
            grid=(16,),
            in_specs=[vmem, pl.BlockSpec((1, 256, 960), lambda i, s: (i, 0, 0))],
            out_specs=pl.BlockSpec((8, GW, 512), lambda i, s: (i, 0, 0)),
            scratch_shapes=[pltpu.VMEM((3, 130, GW, 512), jnp.bfloat16)],
        ),
        cost_estimate=pl.CostEstimate(
            flops=16 * 2 * 256 * 960 * 512, bytes_accessed=16 << 20, transcendentals=0
        ),
        name="conv",
    )(slot, recv, weights)


def solution(mesh):
    placed = (P("fiber", "tm"), P(), P(), P(), P(None, "fiber", None, None, None, None))

    return jax.shard_map(
        shards, mesh=mesh, in_specs=placed, out_specs=P("tm", "fiber", None), check_vma=False
    )
```

```python
import jax
import jax.numpy as jnp
from jax import lax
from jax.experimental import pallas as pl
from jax.experimental.pallas import tpu as pltpu
from jax.sharding import PartitionSpec as P

HOP = 128
GW = 32
AXES = ("tm", "fiber")
TURN = 0


PLACES = [(x, y, z, c) for x in range(4) for y in range(4) for z in range(8) for c in range(2)]


def flat(x, y, z, c):
    return ((y * 4 + z // 2) * 2 + c) * 8 + x * 2 + z % 2


def spot(x, y, late, odd, b, core, early):
    return flat((x - y + TURN - early) % 4, x, 4 * odd + 2 * b + (late ^ odd), core)


def bulk_route(step):
    pairs = []
    for x, y, z, c in PLACES:
        pair, odd = z // 2, z % 2
        late = 0 if pair in (0, 3) else 1
        there = spot(x, y, late, odd, step ^ (pair // 2), c, int(pair == 3))
        pairs.append((flat(x, y, z, c), there))
    return pairs


OTHER_CORE = [(i, i ^ 1) for i in range(32)]


def flip_kernel(taps_ref, out_ref):
    out_ref[...] = taps_ref[...].T


def filter_kernel(where_ref, first_ref, second_ref, other_ref, taps_ref, out_ref, seq_ref, early_ref):
    first, core, keep = where_ref[0], where_ref[1], where_ref[2]
    size = first_ref.shape[1]
    seq_ref[:, 80:96, :] = jnp.zeros((size, 16, HOP), jnp.bfloat16)
    early_ref[...] = jnp.zeros(early_ref.shape, jnp.float32)

    def apply(frames):
        return lax.dot_general(
            taps_ref[...], frames, (((1,), (1,)), ((), ())), preferred_element_type=jnp.float32
        ).astype(jnp.bfloat16)

    for base in range(0, size, 16):
        chans = min(16, size - base)
        rows = slice(base, base + chans)
        parts = (first_ref[core, rows], other_ref[0, rows], second_ref[core, rows], other_ref[1, rows])
        for j, part in enumerate(parts):
            at = (first ^ (j >> 1)) * 48 + (core ^ (j & 1)) * 16
            seq_ref[rows, pl.ds(pl.multiple_of(at, 16), 16), :] = part
        seq_ref[rows, 32:48, :] = seq_ref[rows, 48:64, :] * keep.astype(jnp.bfloat16)
        columns = []
        for k in range(4):
            runs = [seq_ref[rows, s + k : s + k + 32, :] for s in (0, 48)]
            columns.append(jnp.concatenate(runs, axis=1).reshape(chans * 64, HOP))
        feats = apply(jnp.concatenate(columns, axis=1))
        for g in range(8):
            for p in range(chans // 2):
                out_ref[g, base // 2 + p] = feats[
                    g * GW : (g + 1) * GW, p * 128 : (p + 1) * 128
                ]
        for c in range(chans):
            pair, side = (base + c) // 2, c % 2
            at = 128 * (pair // 21) + 64 * side + 3 * (pair % 21)
            head = seq_ref[base + c, 0:3, :].astype(jnp.float32)
            for k in range(1, 4):
                early_ref[at + 3 - k : at + 3, k * HOP : (k + 1) * HOP] = head[:k]
    feats = apply(early_ref[...].astype(jnp.bfloat16))
    for g in range(8):
        for h in range(2):
            out_ref[g, size // 2 + h] = feats[g * GW : (g + 1) * GW, h * 128 : (h + 1) * 128]


def weight_kernel(flag_ref, kern_ref, out_ref, base_ref):
    block = pl.program_id(0)

    @pl.when(block == 0)
    def _():
        r = lax.broadcasted_iota(jnp.int32, (288, 960), 0)
        k = lax.broadcasted_iota(jnp.int32, (288, 960), 1)
        lag = k - r - 224 * ((r >= 96).astype(jnp.int32) + (r >= 192).astype(jnp.int32))
        for c in range(8):
            spread = jnp.where(lag == 32 * c, 1.0, 0.0).astype(jnp.bfloat16)
            base_ref[c] = jnp.dot(kern_ref[...], spread, preferred_element_type=jnp.float32)

    k = lax.broadcasted_iota(jnp.int32, (1, 960), 1)
    k = k - 320 * ((k >= 320).astype(jnp.int32) + (k >= 640).astype(jnp.int32))
    for c in range(8):
        at = block * 8 + c
        low, high = flag_ref[1, at].astype(jnp.float32), flag_ref[2, at].astype(jnp.float32)
        mask = jnp.where(k < 32 * c + 32, low, jnp.where(k >= 32 * c + 64, high, 1.0))
        rows = base_ref[c, pl.ds(pl.multiple_of(flag_ref[0, at] * GW, GW), GW), :]
        out_ref[0, c * GW : (c + 1) * GW, :] = (rows * mask).astype(jnp.bfloat16)


def assemble(x_ref, load, pairs, sides, place):
    size = pairs * GW
    lane = lax.broadcasted_iota(jnp.int16, (size, 128), 1)
    v = [load(q).reshape(size, 128) for q in range(8)]
    near = [pltpu.roll(u, 32, 1) for u in v]
    far = [pltpu.roll(u, 96, 1) for u in v]
    zero = jnp.zeros((size, 128), jnp.bfloat16)
    for side in sides:
        outer, inner = (near, far) if side else (far, near)
        t = [
            jnp.where(
                lane < 32,
                outer[2 * m],
                jnp.where(lane < 96, inner[2 * m + 1], outer[(2 * m + 2) % 8]),
            )
            for m in range(4)
        ]
        back = [pltpu.roll(u, 1, 1) for u in t]
        ahead = [pltpu.roll(u, 127, 1) for u in t]
        for m in range(4):
            before = jnp.where(lane == 0, back[m - 1] if m else zero, back[m])
            after = jnp.where(lane == 127, ahead[m + 1] if m < 3 else zero, ahead[m])
            for e, u in enumerate((before, t[m], after)):
                for p in range(pairs):
                    x_ref[e, place(p, side), :, m * 128 : (m + 1) * 128] = u[
                        p * GW : (p + 1) * GW
                    ]


def multiply(w_ref, x_ref, row, out_ref):
    x = jnp.concatenate(
        [x_ref[e, pl.ds(row, 10)].reshape(10 * GW, 512) for e in range(3)], axis=0
    )
    res = jnp.dot(w_ref[0], x, preferred_element_type=jnp.float32)
    out_ref[...] = res.astype(jnp.bfloat16).reshape(8, GW, 512)


def place_early(late_ref, load, spread_ref):
    for h in range(2):
        rows = jnp.concatenate([load(q, h) for q in range(8)], axis=0)
        for j in range(0, 21, 7):
            res = jnp.dot(
                rows, spread_ref[:, j * 128 : (j + 7) * 128], preferred_element_type=jnp.float32
            ).astype(jnp.bfloat16)
            for k in range(7):
                for q in range(8):
                    late_ref[21 * h + j + k, (q + 7) % 8] = res[
                        q * GW : (q + 1) * GW, k * 128 : (k + 1) * 128
                    ]


def inner_kernel(slot_ref, recv_ref, spread_ref, w_ref, out_ref, side_ref, x_ref, late_ref):
    step = pl.program_id(0)

    @pl.when(step == 0)
    def _():
        place_early(late_ref, lambda q, h: recv_ref[slot_ref[q], 32 + h], spread_ref)

        @pl.loop(0, 8)
        def _(g):
            assemble(
                x_ref,
                lambda q: recv_ref[slot_ref[q], pl.ds(g * 4, 4)] + late_ref[pl.ds(g * 4, 4), q],
                4,
                (0, 1),
                lambda p, side: 8 * g + 2 * p + side,
            )

        for e in range(3):
            side_ref[e, 0:9] = x_ref[e, 0:9]
            side_ref[e, 9:18] = x_ref[e, 55:64]

    multiply(w_ref, x_ref, step * 8 + 7, out_ref)


def outer_kernel(slot_ref, recv_ref, spread_ref, side_ref, w_ref, done_ref, out_ref, x_ref, late_ref):
    step = pl.program_id(0)

    def group(g):
        at = 8 * g + 1 + 18 * (g // 4)
        assemble(
            x_ref,
            lambda q: recv_ref[slot_ref[q], pl.ds(g * 4, 4)] + late_ref[pl.ds(g * 4, 4), q],
            4,
            (0, 1),
            lambda p, side: at + 2 * p + side,
        )

    row = 8 * step + 2 * (step // 5)

    @pl.when(step == 0)
    def _():
        place_early(late_ref, lambda q, h: recv_ref[slot_ref[q], 33 + h], spread_ref)
        for e in range(3):
            x_ref[e, 33:51] = side_ref[e]
        assemble(
            x_ref,
            lambda q: recv_ref[slot_ref[q], 32] + late_ref[32, q],
            1,
            (0, 1),
            lambda p, side: 83 * side,
        )
        group(0)

    @pl.when(step < 7)
    def _():
        group(step + 1)
        multiply(w_ref, x_ref, row, out_ref)

    @pl.when(step >= 7)
    def _():
        multiply(w_ref, x_ref, row, out_ref)


def whole(*shape):
    return pl.BlockSpec(shape, lambda i, s: (0,) * len(shape))


VMEM = pl.BlockSpec(memory_space=pltpu.VMEM)
SMEM = pl.BlockSpec(memory_space=pltpu.SMEM)


def shards(waveform, filters, channel_section, section_bank, conv_bank):
    tm, fiber = lax.axis_index("tm"), lax.axis_index("fiber")
    y, zh, core, x, z0 = tm >> 3, (tm >> 1) & 3, tm & 1, fiber >> 1, fiber & 1
    z2, z1 = zh >> 1, zh & 1
    late = z0 ^ z2
    first = 1 ^ z1 ^ late

    def send(part, perm, axes=AXES):
        return lax.ppermute(part, axes, perm)

    got = ([], [])
    for step in (0, 1):
        rows = lax.dynamic_slice_in_dim(waveform, 256 * (step ^ z2), 256, 0)
        part = rows.reshape(2, 128, 16, HOP)[:, 32:96]
        got[0].append(send(part, bulk_route(step)))
    up = [(i, i + 1) for i in range(7)]
    row_low = send(waveform[511:], up, "fiber")
    row_high = send(waveform[:1], [(j, i) for i, j in up], "fiber")
    wave, row_low, row_high = lax.optimization_barrier((waveform, row_low, row_high))
    sides = [row_low] + [wave[i : i + 1] for i in (128, 127, 256, 255, 384, 383)] + [row_high]
    sides = jnp.concatenate(sides, axis=0).reshape(4, 2, 16, HOP)
    for step in (0, 1):
        rows = lax.dynamic_slice_in_dim(wave, 256 * (step ^ z2), 256, 0)
        rows = rows.reshape(2, 128, 16, HOP)
        extra = lax.dynamic_slice_in_dim(sides, 2 * (step ^ z2), 2, 0)
        part = jnp.concatenate([rows[:, :32], rows[:, 96:], extra], axis=1)
        got[1].append(send(part, bulk_route(step)))

    taps = pl.pallas_call(
        flip_kernel,
        out_shape=jax.ShapeDtypeStruct((256, 512), jnp.bfloat16),
        cost_estimate=pl.CostEstimate(flops=0, bytes_accessed=1 << 19, transcendentals=0),
        name="flip",
    )(filters)

    keep = jnp.where((late == 0) & (((y - x + TURN) & 3) == 0), 0, 1)
    where = jnp.stack([first, core, keep]).astype(jnp.int32)
    recv = []
    for half in (0, 1):
        size = 66 if half else 64
        theirs = [lax.dynamic_index_in_dim(g, 1 - core, 0, False) for g in got[half]]
        other = send(jnp.stack(theirs), OTHER_CORE, "tm")
        feats = pl.pallas_call(
            filter_kernel,
            out_shape=jax.ShapeDtypeStruct((8, size // 2 + 2, GW, 128), jnp.bfloat16),
            in_specs=[SMEM] + [VMEM] * 4,
            out_specs=VMEM,
            scratch_shapes=[
                pltpu.VMEM((size, 96, HOP), jnp.bfloat16),
                pltpu.VMEM((256, 512), jnp.float32),
            ],
            cost_estimate=pl.CostEstimate(
                flops=size * 2 * 64 * 512 * 256, bytes_accessed=size * 49152, transcendentals=0
            ),
            name="filterbank",
        )(where, *got[half], other, taps)
        recv.append(lax.all_to_all(feats, "fiber", 0, 0, tiled=True))

    edge = jnp.array([-1], jnp.int32)
    sec = lax.dynamic_slice_in_dim(
        jnp.concatenate([edge, channel_section, edge]), tm * 128, 130, 0
    )
    middle = sec[1:-1]
    table = lax.dynamic_slice_in_dim(section_bank, fiber, 1, 1)
    onehot = (middle[:, None] == jnp.arange(table.shape[0], dtype=jnp.int32)[None, :]).astype(
        jnp.int32
    )
    choose = jnp.sum(onehot * table[:, 0][None, :], axis=1)
    flags = jnp.stack([choose, sec[:-2] == middle, sec[2:] == middle]).astype(jnp.int32)
    kern = conv_bank[:, 0].transpose(0, 3, 2, 1, 4).reshape(64, 288)
    weights = pl.pallas_call(
        weight_kernel,
        out_shape=jax.ShapeDtypeStruct((16, 256, 960), jnp.bfloat16),
        grid_spec=pltpu.PrefetchScalarGridSpec(
            num_scalar_prefetch=1,
            grid=(16,),
            in_specs=[whole(64, 288)],
            out_specs=pl.BlockSpec((1, 256, 960), lambda i, s: (i, 0, 0)),
            scratch_shapes=[pltpu.VMEM((8, 64, 960), jnp.float32)],
        ),
        cost_estimate=pl.CostEstimate(
            flops=8 * 2 * 64 * 288 * 960, bytes_accessed=8 << 20, transcendentals=0
        ),
        name="weights",
    )(flags, kern)

    q = jnp.arange(8, dtype=jnp.int32)
    slot = (2 * ((y + TURN - (q >> 1)) & 3) + ((q & 1) ^ z2)).astype(jnp.int32)
    at = jnp.arange(21 * 128, dtype=jnp.int32)
    source = jnp.where(at % 64 >= 61, (at % 128) // 64 * 64 + 3 * (at // 128) + at % 64 - 61, -1)
    spread = (jnp.arange(128, dtype=jnp.int32)[:, None] == source[None, :]).astype(jnp.bfloat16)
    late_rows = pltpu.VMEM((42, 8, GW, 128), jnp.bfloat16)
    part, side = pl.pallas_call(
        inner_kernel,
        out_shape=(
            jax.ShapeDtypeStruct((128, GW, 512), jnp.bfloat16),
            jax.ShapeDtypeStruct((3, 18, GW, 512), jnp.bfloat16),
        ),
        grid_spec=pltpu.PrefetchScalarGridSpec(
            num_scalar_prefetch=1,
            grid=(6,),
            in_specs=[
                whole(8, 34, GW, 128),
                whole(128, 21 * 128),
                pl.BlockSpec((1, 256, 960), lambda i, s: (i + 5, 0, 0)),
            ],
            out_specs=(
                pl.BlockSpec((8, GW, 512), lambda i, s: (i + 5, 0, 0)),
                whole(3, 18, GW, 512),
            ),
            scratch_shapes=[pltpu.VMEM((3, 64, GW, 512), jnp.bfloat16), late_rows],
        ),
        cost_estimate=pl.CostEstimate(
            flops=6 * 2 * 256 * 960 * 512, bytes_accessed=8 << 20, transcendentals=0
        ),
        name="conv_inner",
    )(slot, recv[0], spread, weights)
    return pl.pallas_call(
        outer_kernel,
        out_shape=jax.ShapeDtypeStruct((128, GW, 512), jnp.bfloat16),
        grid_spec=pltpu.PrefetchScalarGridSpec(
            num_scalar_prefetch=1,
            grid=(10,),
            in_specs=[
                whole(8, 35, GW, 128),
                whole(128, 21 * 128),
                whole(3, 18, GW, 512),
                pl.BlockSpec((1, 256, 960), lambda i, s: (i + 6 * (i // 5), 0, 0)),
                pl.BlockSpec(memory_space=pl.ANY),
            ],
            out_specs=pl.BlockSpec((8, GW, 512), lambda i, s: (i + 6 * (i // 5), 0, 0)),
            scratch_shapes=[pltpu.VMEM((3, 84, GW, 512), jnp.bfloat16), late_rows],
        ),
        input_output_aliases={5: 0},
        cost_estimate=pl.CostEstimate(
            flops=10 * 2 * 256 * 960 * 512, bytes_accessed=8 << 20, transcendentals=0
        ),
        name="conv_outer",
    )(slot, recv[1], spread, side, weights, part)


def solution(mesh):
    placed = (P("fiber", "tm"), P(), P(), P(), P(None, "fiber", None, None, None, None))

    return jax.shard_map(
        shards, mesh=mesh, in_specs=placed, out_specs=P("tm", "fiber", None), check_vma=False
    )
```

```python
import functools

import jax
import jax.numpy as jnp
from jax import lax
from jax.experimental import pallas as pl
from jax.experimental.pallas import tpu as pltpu
from jax.sharding import PartitionSpec as P

HOP = 128
GW = 32
AXES = ("tm", "fiber")
TURN = 0


PLACES = [(x, y, z, c) for x in range(4) for y in range(4) for z in range(8) for c in range(2)]


def flat(x, y, z, c):
    return ((y * 4 + z // 2) * 2 + c) * 8 + x * 2 + z % 2


def spot(x, y, late, odd, b, core, early):
    return flat((x - y + TURN - early) % 4, x, 4 * odd + 2 * b + (late ^ odd), core)


def bulk_route(step):
    pairs = []
    for x, y, z, c in PLACES:
        pair, odd = z // 2, z % 2
        late = 0 if pair in (0, 3) else 1
        there = spot(x, y, late, odd, step ^ (pair // 2), c, int(pair == 3))
        pairs.append((flat(x, y, z, c), there))
    return pairs


OTHER_CORE = [(i, i ^ 1) for i in range(32)]


def flip_kernel(taps_ref, out_ref):
    out_ref[...] = taps_ref[...].T


def filter_kernel(where_ref, first_ref, second_ref, other_ref, taps_ref, out_ref, seq_ref, early_ref):
    first, core, keep = where_ref[0], where_ref[1], where_ref[2]
    size = first_ref.shape[1]
    seq_ref[:, 80:96, :] = jnp.zeros((size, 16, HOP), jnp.bfloat16)
    early_ref[...] = jnp.zeros(early_ref.shape, jnp.float32)

    def apply(frames):
        return lax.dot_general(
            taps_ref[...], frames, (((1,), (1,)), ((), ())), preferred_element_type=jnp.float32
        ).astype(jnp.bfloat16)

    for base in range(0, size, 16):
        chans = min(16, size - base)
        rows = slice(base, base + chans)
        parts = (first_ref[core, rows], other_ref[0, rows], second_ref[core, rows], other_ref[1, rows])
        for j, part in enumerate(parts):
            at = (first ^ (j >> 1)) * 48 + (core ^ (j & 1)) * 16
            seq_ref[rows, pl.ds(pl.multiple_of(at, 16), 16), :] = part
        seq_ref[rows, 32:48, :] = seq_ref[rows, 48:64, :] * keep.astype(jnp.bfloat16)
        columns = []
        for k in range(4):
            runs = [seq_ref[rows, s + k : s + k + 32, :] for s in (0, 48)]
            columns.append(jnp.concatenate(runs, axis=1).reshape(chans * 64, HOP))
        feats = apply(jnp.concatenate(columns, axis=1))
        for g in range(8):
            for p in range(chans // 2):
                out_ref[g, base // 2 + p] = feats[
                    g * GW : (g + 1) * GW, p * 128 : (p + 1) * 128
                ]
        for c in range(chans):
            pair, side = (base + c) // 2, c % 2
            at = 128 * (pair // 21) + 64 * side + 3 * (pair % 21)
            head = seq_ref[base + c, 0:3, :].astype(jnp.float32)
            for k in range(1, 4):
                early_ref[at + 3 - k : at + 3, k * HOP : (k + 1) * HOP] = head[:k]
    feats = apply(early_ref[...].astype(jnp.bfloat16))
    for g in range(8):
        for h in range(2):
            out_ref[g, size // 2 + h] = feats[g * GW : (g + 1) * GW, h * 128 : (h + 1) * 128]


def weight_kernel(inner, flag_ref, kern_ref, out_ref, base_ref):
    block = pl.program_id(0)

    @pl.when(block == 0)
    def _():
        r = lax.broadcasted_iota(jnp.int32, (288, 960), 0)
        k = lax.broadcasted_iota(jnp.int32, (288, 960), 1)
        lag = k - r - 224 * ((r >= 96).astype(jnp.int32) + (r >= 192).astype(jnp.int32))
        for c in range(8):
            spread = jnp.where(lag == 32 * c, 1.0, 0.0).astype(jnp.bfloat16)
            base_ref[c] = jnp.dot(kern_ref[...], spread, preferred_element_type=jnp.float32)

    k = lax.broadcasted_iota(jnp.int32, (1, 960), 1)
    k = k - 320 * ((k >= 320).astype(jnp.int32) + (k >= 640).astype(jnp.int32))
    for c in range(8):
        at = (block + 5 if inner else block + 6 * (block // 5)) * 8 + c
        low, high = flag_ref[1, at].astype(jnp.float32), flag_ref[2, at].astype(jnp.float32)
        mask = jnp.where(k < 32 * c + 32, low, jnp.where(k >= 32 * c + 64, high, 1.0))
        rows = base_ref[c, pl.ds(pl.multiple_of(flag_ref[0, at] * GW, GW), GW), :]
        out_ref[0, c * GW : (c + 1) * GW, :] = (rows * mask).astype(jnp.bfloat16)


def assemble(x_ref, load, pairs, sides, place):
    size = pairs * GW
    lane = lax.broadcasted_iota(jnp.int16, (size, 128), 1)
    v = [load(q).reshape(size, 128) for q in range(8)]
    near = [pltpu.roll(u, 32, 1) for u in v]
    far = [pltpu.roll(u, 96, 1) for u in v]
    zero = jnp.zeros((size, 128), jnp.bfloat16)
    for side in sides:
        outer, inner = (near, far) if side else (far, near)
        t = [
            jnp.where(
                lane < 32,
                outer[2 * m],
                jnp.where(lane < 96, inner[2 * m + 1], outer[(2 * m + 2) % 8]),
            )
            for m in range(4)
        ]
        back = [pltpu.roll(u, 1, 1) for u in t]
        ahead = [pltpu.roll(u, 127, 1) for u in t]
        for m in range(4):
            before = jnp.where(lane == 0, back[m - 1] if m else zero, back[m])
            after = jnp.where(lane == 127, ahead[m + 1] if m < 3 else zero, ahead[m])
            for e, u in enumerate((before, t[m], after)):
                for p in range(pairs):
                    x_ref[e, place(p, side), :, m * 128 : (m + 1) * 128] = u[
                        p * GW : (p + 1) * GW
                    ]


def multiply(w_ref, x_ref, row, out_ref):
    x = jnp.concatenate(
        [x_ref[e, pl.ds(row, 10)].reshape(10 * GW, 512) for e in range(3)], axis=0
    )
    res = jnp.dot(w_ref[0], x, preferred_element_type=jnp.float32)
    out_ref[...] = res.astype(jnp.bfloat16).reshape(8, GW, 512)


def place_early(late_ref, load, spread_ref):
    for h in range(2):
        rows = jnp.concatenate([load(q, h) for q in range(8)], axis=0)
        for j in range(0, 21, 7):
            res = jnp.dot(
                rows, spread_ref[:, j * 128 : (j + 7) * 128], preferred_element_type=jnp.float32
            ).astype(jnp.bfloat16)
            for k in range(7):
                for q in range(8):
                    late_ref[21 * h + j + k, (q + 7) % 8] = res[
                        q * GW : (q + 1) * GW, k * 128 : (k + 1) * 128
                    ]


def inner_kernel(slot_ref, recv_ref, spread_ref, w_ref, out_ref, side_ref, x_ref, late_ref):
    step = pl.program_id(0)

    @pl.when(step == 0)
    def _():
        place_early(late_ref, lambda q, h: recv_ref[slot_ref[q], 32 + h], spread_ref)

        @pl.loop(0, 8)
        def _(g):
            assemble(
                x_ref,
                lambda q: recv_ref[slot_ref[q], pl.ds(g * 4, 4)] + late_ref[pl.ds(g * 4, 4), q],
                4,
                (0, 1),
                lambda p, side: 8 * g + 2 * p + side,
            )

        for e in range(3):
            side_ref[e, 0:9] = x_ref[e, 0:9]
            side_ref[e, 9:18] = x_ref[e, 55:64]

    multiply(w_ref, x_ref, step * 8 + 7, out_ref)


def outer_kernel(slot_ref, recv_ref, spread_ref, side_ref, w_ref, done_ref, out_ref, x_ref, late_ref):
    step = pl.program_id(0)

    def group(g):
        at = 8 * g + 1 + 18 * (g // 4)
        assemble(
            x_ref,
            lambda q: recv_ref[slot_ref[q], pl.ds(g * 4, 4)] + late_ref[pl.ds(g * 4, 4), q],
            4,
            (0, 1),
            lambda p, side: at + 2 * p + side,
        )

    row = 8 * step + 2 * (step // 5)

    @pl.when(step == 0)
    def _():
        place_early(late_ref, lambda q, h: recv_ref[slot_ref[q], 33 + h], spread_ref)
        for e in range(3):
            x_ref[e, 33:51] = side_ref[e]
        assemble(
            x_ref,
            lambda q: recv_ref[slot_ref[q], 32] + late_ref[32, q],
            1,
            (0, 1),
            lambda p, side: 83 * side,
        )
        group(0)

    @pl.when(step < 7)
    def _():
        group(step + 1)
        multiply(w_ref, x_ref, row, out_ref)

    @pl.when(step >= 7)
    def _():
        multiply(w_ref, x_ref, row, out_ref)


def whole(*shape):
    return pl.BlockSpec(shape, lambda i, s: (0,) * len(shape))


VMEM = pl.BlockSpec(memory_space=pltpu.VMEM)
SMEM = pl.BlockSpec(memory_space=pltpu.SMEM)


def shards(waveform, filters, channel_section, section_bank, conv_bank):
    tm, fiber = lax.axis_index("tm"), lax.axis_index("fiber")
    y, zh, core, x, z0 = tm >> 3, (tm >> 1) & 3, tm & 1, fiber >> 1, fiber & 1
    z2, z1 = zh >> 1, zh & 1
    late = z0 ^ z2
    first = 1 ^ z1 ^ late

    def send(part, perm, axes=AXES):
        return lax.ppermute(part, axes, perm)

    got = ([], [])
    for step in (0, 1):
        rows = lax.dynamic_slice_in_dim(waveform, 256 * (step ^ z2), 256, 0)
        part = rows.reshape(2, 128, 16, HOP)[:, 32:96]
        got[0].append(send(part, bulk_route(step)))
    up = [(i, i + 1) for i in range(7)]
    row_low = send(waveform[511:], up, "fiber")
    row_high = send(waveform[:1], [(j, i) for i, j in up], "fiber")
    wave, row_low, row_high = lax.optimization_barrier((waveform, row_low, row_high))
    sides = [row_low] + [wave[i : i + 1] for i in (128, 127, 256, 255, 384, 383)] + [row_high]
    sides = jnp.concatenate(sides, axis=0).reshape(4, 2, 16, HOP)
    for step in (0, 1):
        rows = lax.dynamic_slice_in_dim(wave, 256 * (step ^ z2), 256, 0)
        rows = rows.reshape(2, 128, 16, HOP)
        extra = lax.dynamic_slice_in_dim(sides, 2 * (step ^ z2), 2, 0)
        part = jnp.concatenate([rows[:, :32], rows[:, 96:], extra], axis=1)
        got[1].append(send(part, bulk_route(step)))

    taps = pl.pallas_call(
        flip_kernel,
        out_shape=jax.ShapeDtypeStruct((256, 512), jnp.bfloat16),
        cost_estimate=pl.CostEstimate(flops=0, bytes_accessed=1 << 19, transcendentals=0),
        name="flip",
    )(filters)

    keep = jnp.where((late == 0) & (((y - x + TURN) & 3) == 0), 0, 1)
    where = jnp.stack([first, core, keep]).astype(jnp.int32)
    recv = []
    for half in (0, 1):
        size = 66 if half else 64
        theirs = [lax.dynamic_index_in_dim(g, 1 - core, 0, False) for g in got[half]]
        other = send(jnp.stack(theirs), OTHER_CORE, "tm")
        feats = pl.pallas_call(
            filter_kernel,
            out_shape=jax.ShapeDtypeStruct((8, size // 2 + 2, GW, 128), jnp.bfloat16),
            in_specs=[SMEM] + [VMEM] * 4,
            out_specs=VMEM,
            scratch_shapes=[
                pltpu.VMEM((size, 96, HOP), jnp.bfloat16),
                pltpu.VMEM((256, 512), jnp.float32),
            ],
            cost_estimate=pl.CostEstimate(
                flops=size * 2 * 64 * 512 * 256, bytes_accessed=size * 49152, transcendentals=0
            ),
            name="filterbank",
        )(where, *got[half], other, taps)
        recv.append(lax.all_to_all(feats, "fiber", 0, 0, tiled=True))

    edge = jnp.array([-1], jnp.int32)
    sec = lax.dynamic_slice_in_dim(
        jnp.concatenate([edge, channel_section, edge]), tm * 128, 130, 0
    )
    middle = sec[1:-1]
    table = lax.dynamic_slice_in_dim(section_bank, fiber, 1, 1)
    onehot = (middle[:, None] == jnp.arange(table.shape[0], dtype=jnp.int32)[None, :]).astype(
        jnp.int32
    )
    choose = jnp.sum(onehot * table[:, 0][None, :], axis=1)
    flags = jnp.stack([choose, sec[:-2] == middle, sec[2:] == middle]).astype(jnp.int32)
    kern = conv_bank[:, 0].transpose(0, 3, 2, 1, 4).reshape(64, 288)

    def weights(inner):
        count = 6 if inner else 10
        return pl.pallas_call(
            functools.partial(weight_kernel, inner),
            out_shape=jax.ShapeDtypeStruct((count, 256, 960), jnp.bfloat16),
            grid_spec=pltpu.PrefetchScalarGridSpec(
                num_scalar_prefetch=1,
                grid=(count,),
                in_specs=[whole(64, 288)],
                out_specs=pl.BlockSpec((1, 256, 960), lambda i, s: (i, 0, 0)),
                scratch_shapes=[pltpu.VMEM((8, 64, 960), jnp.float32)],
            ),
            cost_estimate=pl.CostEstimate(
                flops=8 * 2 * 64 * 288 * 960, bytes_accessed=4 << 20, transcendentals=0
            ),
            name="weights",
        )(flags, kern)

    inner_weights, outer_weights = weights(True), weights(False)
    q = jnp.arange(8, dtype=jnp.int32)
    slot = (2 * ((y + TURN - (q >> 1)) & 3) + ((q & 1) ^ z2)).astype(jnp.int32)
    at = jnp.arange(21 * 128, dtype=jnp.int32)
    source = jnp.where(at % 64 >= 61, (at % 128) // 64 * 64 + 3 * (at // 128) + at % 64 - 61, -1)
    spread = (jnp.arange(128, dtype=jnp.int32)[:, None] == source[None, :]).astype(jnp.bfloat16)
    late_rows = pltpu.VMEM((42, 8, GW, 128), jnp.bfloat16)
    part, side = pl.pallas_call(
        inner_kernel,
        out_shape=(
            jax.ShapeDtypeStruct((128, GW, 512), jnp.bfloat16),
            jax.ShapeDtypeStruct((3, 18, GW, 512), jnp.bfloat16),
        ),
        grid_spec=pltpu.PrefetchScalarGridSpec(
            num_scalar_prefetch=1,
            grid=(6,),
            in_specs=[
                whole(8, 34, GW, 128),
                whole(128, 21 * 128),
                pl.BlockSpec((1, 256, 960), lambda i, s: (i, 0, 0)),
            ],
            out_specs=(
                pl.BlockSpec((8, GW, 512), lambda i, s: (i + 5, 0, 0)),
                whole(3, 18, GW, 512),
            ),
            scratch_shapes=[pltpu.VMEM((3, 64, GW, 512), jnp.bfloat16), late_rows],
        ),
        cost_estimate=pl.CostEstimate(
            flops=6 * 2 * 256 * 960 * 512, bytes_accessed=8 << 20, transcendentals=0
        ),
        name="conv_inner",
    )(slot, recv[0], spread, inner_weights)
    return pl.pallas_call(
        outer_kernel,
        out_shape=jax.ShapeDtypeStruct((128, GW, 512), jnp.bfloat16),
        grid_spec=pltpu.PrefetchScalarGridSpec(
            num_scalar_prefetch=1,
            grid=(10,),
            in_specs=[
                whole(8, 35, GW, 128),
                whole(128, 21 * 128),
                whole(3, 18, GW, 512),
                pl.BlockSpec((1, 256, 960), lambda i, s: (i, 0, 0)),
                pl.BlockSpec(memory_space=pl.ANY),
            ],
            out_specs=pl.BlockSpec((8, GW, 512), lambda i, s: (i + 6 * (i // 5), 0, 0)),
            scratch_shapes=[pltpu.VMEM((3, 84, GW, 512), jnp.bfloat16), late_rows],
        ),
        input_output_aliases={5: 0},
        cost_estimate=pl.CostEstimate(
            flops=10 * 2 * 256 * 960 * 512, bytes_accessed=8 << 20, transcendentals=0
        ),
        name="conv_outer",
    )(slot, recv[1], spread, side, outer_weights, part)


def solution(mesh):
    placed = (P("fiber", "tm"), P(), P(), P(), P(None, "fiber", None, None, None, None))

    return jax.shard_map(
        shards, mesh=mesh, in_specs=placed, out_specs=P("tm", "fiber", None), check_vma=False
    )
```

```python
import jax
import jax.numpy as jnp
from jax import lax
from jax.experimental import pallas as pl
from jax.experimental.pallas import tpu as pltpu
from jax.sharding import PartitionSpec as P

HOP = 128
GW = 32
AXES = ("tm", "fiber")
TURN = (0, 2)


PLACES = [(x, y, z, c) for x in range(4) for y in range(4) for z in range(8) for c in range(2)]


def flat(x, y, z, c):
    return ((y * 4 + z // 2) * 2 + c) * 8 + x * 2 + z % 2


def spot(x, y, late, odd, b, core, early, turn):
    return flat((x - y + turn - early) % 4, x, 4 * odd + 2 * b + (late ^ odd), core)


def bulk_route(step, turn):
    pairs = []
    for x, y, z, c in PLACES:
        pair, odd = z // 2, z % 2
        late = 0 if pair in (0, 3) else 1
        there = spot(x, y, late, odd, step ^ (pair // 2), c, int(pair == 3), turn)
        pairs.append((flat(x, y, z, c), there))
    return pairs


OTHER_CORE = [(i, i ^ 1) for i in range(32)]


def flip_kernel(taps_ref, out_ref):
    out_ref[...] = taps_ref[...].T


def filter_kernel(where_ref, first_ref, second_ref, other_ref, taps_ref, out_ref, seq_ref, early_ref):
    first, core, keep = where_ref[0], where_ref[1], where_ref[2]
    size = first_ref.shape[1]
    seq_ref[:, 80:96, :] = jnp.zeros((size, 16, HOP), jnp.bfloat16)
    early_ref[...] = jnp.zeros(early_ref.shape, jnp.float32)

    def apply(frames):
        return lax.dot_general(
            taps_ref[...], frames, (((1,), (1,)), ((), ())), preferred_element_type=jnp.float32
        ).astype(jnp.bfloat16)

    for base in range(0, size, 16):
        chans = min(16, size - base)
        rows = slice(base, base + chans)
        parts = (first_ref[core, rows], other_ref[0, rows], second_ref[core, rows], other_ref[1, rows])
        for j, part in enumerate(parts):
            at = (first ^ (j >> 1)) * 48 + (core ^ (j & 1)) * 16
            seq_ref[rows, pl.ds(pl.multiple_of(at, 16), 16), :] = part
        seq_ref[rows, 32:48, :] = seq_ref[rows, 48:64, :] * keep.astype(jnp.bfloat16)
        columns = []
        for k in range(4):
            runs = [seq_ref[rows, s + k : s + k + 32, :] for s in (0, 48)]
            columns.append(jnp.concatenate(runs, axis=1).reshape(chans * 64, HOP))
        feats = apply(jnp.concatenate(columns, axis=1))
        for g in range(8):
            for p in range(chans // 2):
                out_ref[g, base // 2 + p] = feats[
                    g * GW : (g + 1) * GW, p * 128 : (p + 1) * 128
                ]
        for c in range(chans):
            pair, side = (base + c) // 2, c % 2
            at = 128 * (pair // 21) + 64 * side + 3 * (pair % 21)
            head = seq_ref[base + c, 0:3, :].astype(jnp.float32)
            for k in range(1, 4):
                early_ref[at + 3 - k : at + 3, k * HOP : (k + 1) * HOP] = head[:k]
    feats = apply(early_ref[...].astype(jnp.bfloat16))
    for g in range(8):
        for h in range(2):
            out_ref[g, size // 2 + h] = feats[g * GW : (g + 1) * GW, h * 128 : (h + 1) * 128]


def weight_kernel(flag_ref, kern_ref, out_ref, base_ref):
    block = pl.program_id(0)

    @pl.when(block == 0)
    def _():
        r = lax.broadcasted_iota(jnp.int32, (288, 960), 0)
        k = lax.broadcasted_iota(jnp.int32, (288, 960), 1)
        lag = k - r - 224 * ((r >= 96).astype(jnp.int32) + (r >= 192).astype(jnp.int32))
        for c in range(8):
            spread = jnp.where(lag == 32 * c, 1.0, 0.0).astype(jnp.bfloat16)
            base_ref[c] = jnp.dot(kern_ref[...], spread, preferred_element_type=jnp.float32)

    k = lax.broadcasted_iota(jnp.int32, (1, 960), 1)
    k = k - 320 * ((k >= 320).astype(jnp.int32) + (k >= 640).astype(jnp.int32))
    for c in range(8):
        at = block * 8 + c
        low, high = flag_ref[1, at].astype(jnp.float32), flag_ref[2, at].astype(jnp.float32)
        mask = jnp.where(k < 32 * c + 32, low, jnp.where(k >= 32 * c + 64, high, 1.0))
        rows = base_ref[c, pl.ds(pl.multiple_of(flag_ref[0, at] * GW, GW), GW), :]
        out_ref[0, c * GW : (c + 1) * GW, :] = (rows * mask).astype(jnp.bfloat16)


def assemble(x_ref, load, pairs, sides, place):
    size = pairs * GW
    lane = lax.broadcasted_iota(jnp.int16, (size, 128), 1)
    v = [load(q).reshape(size, 128) for q in range(8)]
    near = [pltpu.roll(u, 32, 1) for u in v]
    far = [pltpu.roll(u, 96, 1) for u in v]
    zero = jnp.zeros((size, 128), jnp.bfloat16)
    for side in sides:
        outer, inner = (near, far) if side else (far, near)
        t = [
            jnp.where(
                lane < 32,
                outer[2 * m],
                jnp.where(lane < 96, inner[2 * m + 1], outer[(2 * m + 2) % 8]),
            )
            for m in range(4)
        ]
        back = [pltpu.roll(u, 1, 1) for u in t]
        ahead = [pltpu.roll(u, 127, 1) for u in t]
        for m in range(4):
            before = jnp.where(lane == 0, back[m - 1] if m else zero, back[m])
            after = jnp.where(lane == 127, ahead[m + 1] if m < 3 else zero, ahead[m])
            for e, u in enumerate((before, t[m], after)):
                for p in range(pairs):
                    x_ref[e, place(p, side), :, m * 128 : (m + 1) * 128] = u[
                        p * GW : (p + 1) * GW
                    ]


def multiply(w_ref, x_ref, row, out_ref):
    x = jnp.concatenate(
        [x_ref[e, pl.ds(row, 10)].reshape(10 * GW, 512) for e in range(3)], axis=0
    )
    res = jnp.dot(w_ref[0], x, preferred_element_type=jnp.float32)
    out_ref[...] = res.astype(jnp.bfloat16).reshape(8, GW, 512)


def place_early(late_ref, load, spread_ref):
    for h in range(2):
        rows = jnp.concatenate([load(q, h) for q in range(8)], axis=0)
        for j in range(0, 21, 7):
            res = jnp.dot(
                rows, spread_ref[:, j * 128 : (j + 7) * 128], preferred_element_type=jnp.float32
            ).astype(jnp.bfloat16)
            for k in range(7):
                for q in range(8):
                    late_ref[21 * h + j + k, (q + 7) % 8] = res[
                        q * GW : (q + 1) * GW, k * 128 : (k + 1) * 128
                    ]


def inner_kernel(slot_ref, recv_ref, spread_ref, w_ref, out_ref, side_ref, x_ref, late_ref):
    step = pl.program_id(0)

    @pl.when(step == 0)
    def _():
        place_early(late_ref, lambda q, h: recv_ref[slot_ref[q], 32 + h], spread_ref)

        @pl.loop(0, 8)
        def _(g):
            assemble(
                x_ref,
                lambda q: recv_ref[slot_ref[q], pl.ds(g * 4, 4)] + late_ref[pl.ds(g * 4, 4), q],
                4,
                (0, 1),
                lambda p, side: 8 * g + 2 * p + side,
            )

        for e in range(3):
            side_ref[e, 0:9] = x_ref[e, 0:9]
            side_ref[e, 9:18] = x_ref[e, 55:64]

    multiply(w_ref, x_ref, step * 8 + 7, out_ref)


def outer_kernel(slot_ref, recv_ref, spread_ref, side_ref, w_ref, done_ref, out_ref, x_ref, late_ref):
    step = pl.program_id(0)

    def group(g):
        at = 8 * g + 1 + 18 * (g // 4)
        assemble(
            x_ref,
            lambda q: recv_ref[slot_ref[q], pl.ds(g * 4, 4)] + late_ref[pl.ds(g * 4, 4), q],
            4,
            (0, 1),
            lambda p, side: at + 2 * p + side,
        )

    row = 8 * step + 2 * (step // 5)

    @pl.when(step == 0)
    def _():
        place_early(late_ref, lambda q, h: recv_ref[slot_ref[q], 33 + h], spread_ref)
        for e in range(3):
            x_ref[e, 33:51] = side_ref[e]
        assemble(
            x_ref,
            lambda q: recv_ref[slot_ref[q], 32] + late_ref[32, q],
            1,
            (0, 1),
            lambda p, side: 83 * side,
        )
        group(0)

    @pl.when(step < 7)
    def _():
        group(step + 1)
        multiply(w_ref, x_ref, row, out_ref)

    @pl.when(step >= 7)
    def _():
        multiply(w_ref, x_ref, row, out_ref)


def whole(*shape):
    return pl.BlockSpec(shape, lambda i, s: (0,) * len(shape))


VMEM = pl.BlockSpec(memory_space=pltpu.VMEM)
SMEM = pl.BlockSpec(memory_space=pltpu.SMEM)


def shards(waveform, filters, channel_section, section_bank, conv_bank):
    tm, fiber = lax.axis_index("tm"), lax.axis_index("fiber")
    y, zh, core, x, z0 = tm >> 3, (tm >> 1) & 3, tm & 1, fiber >> 1, fiber & 1
    z2, z1 = zh >> 1, zh & 1
    late = z0 ^ z2
    first = 1 ^ z1 ^ late

    def send(part, perm, axes=AXES):
        return lax.ppermute(part, axes, perm)

    got = ([], [])
    for step in (0, 1):
        rows = lax.dynamic_slice_in_dim(waveform, 256 * (step ^ z2), 256, 0)
        part = rows.reshape(2, 128, 16, HOP)[:, 32:96]
        got[0].append(send(part, bulk_route(step, TURN[0])))
    up = [(i, i + 1) for i in range(7)]
    row_low = send(waveform[511:], up, "fiber")
    row_high = send(waveform[:1], [(j, i) for i, j in up], "fiber")
    wave, row_low, row_high = lax.optimization_barrier((waveform, row_low, row_high))
    sides = [row_low] + [wave[i : i + 1] for i in (128, 127, 256, 255, 384, 383)] + [row_high]
    sides = jnp.concatenate(sides, axis=0).reshape(4, 2, 16, HOP)
    for step in (0, 1):
        rows = lax.dynamic_slice_in_dim(wave, 256 * (step ^ z2), 256, 0)
        rows = rows.reshape(2, 128, 16, HOP)
        extra = lax.dynamic_slice_in_dim(sides, 2 * (step ^ z2), 2, 0)
        part = jnp.concatenate([rows[:, :32], rows[:, 96:], extra], axis=1)
        got[1].append(send(part, bulk_route(step, TURN[1])))

    taps = pl.pallas_call(
        flip_kernel,
        out_shape=jax.ShapeDtypeStruct((256, 512), jnp.bfloat16),
        cost_estimate=pl.CostEstimate(flops=0, bytes_accessed=1 << 19, transcendentals=0),
        name="flip",
    )(filters)

    recv = []
    for half in (0, 1):
        size = 66 if half else 64
        keep = jnp.where((late == 0) & (((y - x + TURN[half]) & 3) == 0), 0, 1)
        where = jnp.stack([first, core, keep]).astype(jnp.int32)
        theirs = [lax.dynamic_index_in_dim(g, 1 - core, 0, False) for g in got[half]]
        other = send(jnp.stack(theirs), OTHER_CORE, "tm")
        feats = pl.pallas_call(
            filter_kernel,
            out_shape=jax.ShapeDtypeStruct((8, size // 2 + 2, GW, 128), jnp.bfloat16),
            in_specs=[SMEM] + [VMEM] * 4,
            out_specs=VMEM,
            scratch_shapes=[
                pltpu.VMEM((size, 96, HOP), jnp.bfloat16),
                pltpu.VMEM((256, 512), jnp.float32),
            ],
            cost_estimate=pl.CostEstimate(
                flops=size * 2 * 64 * 512 * 256, bytes_accessed=size * 49152, transcendentals=0
            ),
            name="filterbank",
        )(where, *got[half], other, taps)
        recv.append(lax.all_to_all(feats, "fiber", 0, 0, tiled=True))

    edge = jnp.array([-1], jnp.int32)
    sec = lax.dynamic_slice_in_dim(
        jnp.concatenate([edge, channel_section, edge]), tm * 128, 130, 0
    )
    middle = sec[1:-1]
    table = lax.dynamic_slice_in_dim(section_bank, fiber, 1, 1)
    onehot = (middle[:, None] == jnp.arange(table.shape[0], dtype=jnp.int32)[None, :]).astype(
        jnp.int32
    )
    choose = jnp.sum(onehot * table[:, 0][None, :], axis=1)
    flags = jnp.stack([choose, sec[:-2] == middle, sec[2:] == middle]).astype(jnp.int32)
    kern = conv_bank[:, 0].transpose(0, 3, 2, 1, 4).reshape(64, 288)
    weights = pl.pallas_call(
        weight_kernel,
        out_shape=jax.ShapeDtypeStruct((16, 256, 960), jnp.bfloat16),
        grid_spec=pltpu.PrefetchScalarGridSpec(
            num_scalar_prefetch=1,
            grid=(16,),
            in_specs=[whole(64, 288)],
            out_specs=pl.BlockSpec((1, 256, 960), lambda i, s: (i, 0, 0)),
            scratch_shapes=[pltpu.VMEM((8, 64, 960), jnp.float32)],
        ),
        cost_estimate=pl.CostEstimate(
            flops=8 * 2 * 64 * 288 * 960, bytes_accessed=8 << 20, transcendentals=0
        ),
        name="weights",
    )(flags, kern)

    q = jnp.arange(8, dtype=jnp.int32)
    slot = [
        (2 * ((y + turn - (q >> 1)) & 3) + ((q & 1) ^ z2)).astype(jnp.int32) for turn in TURN
    ]
    at = jnp.arange(21 * 128, dtype=jnp.int32)
    source = jnp.where(at % 64 >= 61, (at % 128) // 64 * 64 + 3 * (at // 128) + at % 64 - 61, -1)
    spread = (jnp.arange(128, dtype=jnp.int32)[:, None] == source[None, :]).astype(jnp.bfloat16)
    late_rows = pltpu.VMEM((42, 8, GW, 128), jnp.bfloat16)
    part, side = pl.pallas_call(
        inner_kernel,
        out_shape=(
            jax.ShapeDtypeStruct((128, GW, 512), jnp.bfloat16),
            jax.ShapeDtypeStruct((3, 18, GW, 512), jnp.bfloat16),
        ),
        grid_spec=pltpu.PrefetchScalarGridSpec(
            num_scalar_prefetch=1,
            grid=(6,),
            in_specs=[
                whole(8, 34, GW, 128),
                whole(128, 21 * 128),
                pl.BlockSpec((1, 256, 960), lambda i, s: (i + 5, 0, 0)),
            ],
            out_specs=(
                pl.BlockSpec((8, GW, 512), lambda i, s: (i + 5, 0, 0)),
                whole(3, 18, GW, 512),
            ),
            scratch_shapes=[pltpu.VMEM((3, 64, GW, 512), jnp.bfloat16), late_rows],
        ),
        cost_estimate=pl.CostEstimate(
            flops=6 * 2 * 256 * 960 * 512, bytes_accessed=8 << 20, transcendentals=0
        ),
        name="conv_inner",
    )(slot[0], recv[0], spread, weights)
    return pl.pallas_call(
        outer_kernel,
        out_shape=jax.ShapeDtypeStruct((128, GW, 512), jnp.bfloat16),
        grid_spec=pltpu.PrefetchScalarGridSpec(
            num_scalar_prefetch=1,
            grid=(10,),
            in_specs=[
                whole(8, 35, GW, 128),
                whole(128, 21 * 128),
                whole(3, 18, GW, 512),
                pl.BlockSpec((1, 256, 960), lambda i, s: (i + 6 * (i // 5), 0, 0)),
                pl.BlockSpec(memory_space=pl.ANY),
            ],
            out_specs=pl.BlockSpec((8, GW, 512), lambda i, s: (i + 6 * (i // 5), 0, 0)),
            scratch_shapes=[pltpu.VMEM((3, 84, GW, 512), jnp.bfloat16), late_rows],
        ),
        input_output_aliases={5: 0},
        cost_estimate=pl.CostEstimate(
            flops=10 * 2 * 256 * 960 * 512, bytes_accessed=8 << 20, transcendentals=0
        ),
        name="conv_outer",
    )(slot[1], recv[1], spread, side, weights, part)


def solution(mesh):
    placed = (P("fiber", "tm"), P(), P(), P(), P(None, "fiber", None, None, None, None))

    return jax.shard_map(
        shards, mesh=mesh, in_specs=placed, out_specs=P("tm", "fiber", None), check_vma=False
    )
```

```python
import jax
import jax.numpy as jnp
from jax import lax
from jax.experimental import pallas as pl
from jax.experimental.pallas import tpu as pltpu
from jax.sharding import PartitionSpec as P

HOP = 128
GW = 32
AXES = ("tm", "fiber")
TURN = 0


PLACES = [(x, y, z, c) for x in range(4) for y in range(4) for z in range(8) for c in range(2)]


def flat(x, y, z, c):
    return ((y * 4 + z // 2) * 2 + c) * 8 + x * 2 + z % 2


def spot(x, y, late, odd, b, core, early):
    return flat((x - y + TURN - early) % 4, x, 4 * odd + 2 * b + (late ^ odd), core)


def bulk_route(step):
    pairs = []
    for x, y, z, c in PLACES:
        pair, odd = z // 2, z % 2
        late = 0 if pair in (0, 3) else 1
        there = spot(x, y, late, odd, step ^ (pair // 2), c, int(pair == 3))
        pairs.append((flat(x, y, z, c), there))
    return pairs


OTHER_CORE = [(i, i ^ 1) for i in range(32)]


def flip_kernel(taps_ref, out_ref):
    out_ref[...] = taps_ref[...].T


def filter_kernel(where_ref, first_ref, second_ref, other_ref, taps_ref, out_ref, seq_ref, early_ref):
    first, core, keep = where_ref[0], where_ref[1], where_ref[2]
    size = first_ref.shape[1]
    seq_ref[:, 80:96, :] = jnp.zeros((size, 16, HOP), jnp.bfloat16)
    early_ref[...] = jnp.zeros(early_ref.shape, jnp.float32)

    def apply(frames):
        return lax.dot_general(
            taps_ref[...], frames, (((1,), (1,)), ((), ())), preferred_element_type=jnp.float32
        ).astype(jnp.bfloat16)

    for base in range(0, size, 16):
        chans = min(16, size - base)
        rows = slice(base, base + chans)
        parts = (first_ref[core, rows], other_ref[0, rows], second_ref[core, rows], other_ref[1, rows])
        for j, part in enumerate(parts):
            at = (first ^ (j >> 1)) * 48 + (core ^ (j & 1)) * 16
            seq_ref[rows, pl.ds(pl.multiple_of(at, 16), 16), :] = part
        seq_ref[rows, 32:48, :] = seq_ref[rows, 48:64, :] * keep.astype(jnp.bfloat16)
        columns = []
        for k in range(4):
            runs = [seq_ref[rows, s + k : s + k + 32, :] for s in (0, 48)]
            columns.append(jnp.concatenate(runs, axis=1).reshape(chans * 64, HOP))
        feats = apply(jnp.concatenate(columns, axis=1))
        for g in range(8):
            for p in range(chans // 2):
                out_ref[g, base // 2 + p] = feats[
                    g * GW : (g + 1) * GW, p * 128 : (p + 1) * 128
                ]
        for c in range(chans):
            pair, side = (base + c) // 2, c % 2
            at = 128 * (pair // 21) + 64 * side + 3 * (pair % 21)
            head = seq_ref[base + c, 0:3, :].astype(jnp.float32)
            for k in range(1, 4):
                early_ref[at + 3 - k : at + 3, k * HOP : (k + 1) * HOP] = head[:k]
    feats = apply(early_ref[...].astype(jnp.bfloat16))
    for g in range(8):
        for h in range(2):
            out_ref[g, size // 2 + h] = feats[g * GW : (g + 1) * GW, h * 128 : (h + 1) * 128]


def weight_kernel(flag_ref, kern_ref, out_ref, base_ref):
    block = pl.program_id(0)

    @pl.when(block == 0)
    def _():
        r = lax.broadcasted_iota(jnp.int32, (288, 960), 0)
        k = lax.broadcasted_iota(jnp.int32, (288, 960), 1)
        lag = k - r - 224 * ((r >= 96).astype(jnp.int32) + (r >= 192).astype(jnp.int32))
        for c in range(8):
            spread = jnp.where(lag == 32 * c, 1.0, 0.0).astype(jnp.bfloat16)
            base_ref[c] = jnp.dot(kern_ref[...], spread, preferred_element_type=jnp.float32)

    k = lax.broadcasted_iota(jnp.int32, (1, 960), 1)
    k = k - 320 * ((k >= 320).astype(jnp.int32) + (k >= 640).astype(jnp.int32))
    for c in range(8):
        at = block * 8 + c
        low, high = flag_ref[1, at].astype(jnp.float32), flag_ref[2, at].astype(jnp.float32)
        mask = jnp.where(k < 32 * c + 32, low, jnp.where(k >= 32 * c + 64, high, 1.0))
        rows = base_ref[c, pl.ds(pl.multiple_of(flag_ref[0, at] * GW, GW), GW), :]
        out_ref[0, c * GW : (c + 1) * GW, :] = (rows * mask).astype(jnp.bfloat16)


def assemble(x_ref, load, pairs, sides, place):
    size = pairs * GW
    lane = lax.broadcasted_iota(jnp.int16, (size, 128), 1)
    v = [load(q).reshape(size, 128) for q in range(8)]
    near = [pltpu.roll(u, 32, 1) for u in v]
    far = [pltpu.roll(u, 96, 1) for u in v]
    zero = jnp.zeros((size, 128), jnp.bfloat16)
    for side in sides:
        outer, inner = (near, far) if side else (far, near)
        t = [
            jnp.where(
                lane < 32,
                outer[2 * m],
                jnp.where(lane < 96, inner[2 * m + 1], outer[(2 * m + 2) % 8]),
            )
            for m in range(4)
        ]
        back = [pltpu.roll(u, 1, 1) for u in t]
        ahead = [pltpu.roll(u, 127, 1) for u in t]
        for m in range(4):
            before = jnp.where(lane == 0, back[m - 1] if m else zero, back[m])
            after = jnp.where(lane == 127, ahead[m + 1] if m < 3 else zero, ahead[m])
            for e, u in enumerate((before, t[m], after)):
                for p in range(pairs):
                    x_ref[e, place(p, side), :, m * 128 : (m + 1) * 128] = u[
                        p * GW : (p + 1) * GW
                    ]


def multiply(w_ref, x_ref, row, out_ref):
    x = jnp.concatenate(
        [x_ref[e, pl.ds(row, 10)].reshape(10 * GW, 512) for e in range(3)], axis=0
    )
    res = jnp.dot(w_ref[0], x, preferred_element_type=jnp.float32)
    out_ref[...] = res.astype(jnp.bfloat16).reshape(8, GW, 512)


def place_early(late_ref, load, spread_ref):
    for h in range(2):
        rows = jnp.concatenate([load(q, h) for q in range(8)], axis=0)
        for j in range(0, 21, 7):
            res = jnp.dot(
                rows, spread_ref[:, j * 128 : (j + 7) * 128], preferred_element_type=jnp.float32
            ).astype(jnp.bfloat16)
            for k in range(7):
                for q in range(8):
                    late_ref[21 * h + j + k, (q + 7) % 8] = res[
                        q * GW : (q + 1) * GW, k * 128 : (k + 1) * 128
                    ]


def inner_kernel(slot_ref, recv_ref, spread_ref, w_ref, out_ref, side_ref, x_ref, late_ref):
    step = pl.program_id(0)

    @pl.when(step == 0)
    def _():
        place_early(late_ref, lambda q, h: recv_ref[slot_ref[q], 24 + h], spread_ref)

        @pl.loop(0, 6)
        def _(g):
            assemble(
                x_ref,
                lambda q: recv_ref[slot_ref[q], pl.ds(g * 4, 4)] + late_ref[pl.ds(g * 4, 4), q],
                4,
                (0, 1),
                lambda p, side: 8 * g + 2 * p + side,
            )

        for e in range(3):
            side_ref[e, 0:9] = x_ref[e, 0:9]
            side_ref[e, 9:18] = x_ref[e, 39:48]

    multiply(w_ref, x_ref, step * 8 + 7, out_ref)


def outer_kernel(slot_ref, recv_ref, spread_ref, side_ref, w_ref, done_ref, out_ref, x_ref, late_ref):
    step = pl.program_id(0)

    def group(g):
        at = 8 * g + 1 + 18 * (g // 5)
        assemble(
            x_ref,
            lambda q: recv_ref[slot_ref[q], pl.ds(g * 4, 4)] + late_ref[pl.ds(g * 4, 4), q],
            4,
            (0, 1),
            lambda p, side: at + 2 * p + side,
        )

    row = 8 * step + 2 * (step // 6)

    @pl.when(step == 0)
    def _():
        place_early(late_ref, lambda q, h: recv_ref[slot_ref[q], 41 + h], spread_ref)
        for e in range(3):
            x_ref[e, 41:59] = side_ref[e]
        assemble(
            x_ref,
            lambda q: recv_ref[slot_ref[q], 40] + late_ref[40, q],
            1,
            (0, 1),
            lambda p, side: 99 * side,
        )
        group(0)

    @pl.when(step < 9)
    def _():
        group(step + 1)
        multiply(w_ref, x_ref, row, out_ref)

    @pl.when(step >= 9)
    def _():
        multiply(w_ref, x_ref, row, out_ref)


def whole(*shape):
    return pl.BlockSpec(shape, lambda i, s: (0,) * len(shape))


VMEM = pl.BlockSpec(memory_space=pltpu.VMEM)
SMEM = pl.BlockSpec(memory_space=pltpu.SMEM)


def shards(waveform, filters, channel_section, section_bank, conv_bank):
    tm, fiber = lax.axis_index("tm"), lax.axis_index("fiber")
    y, zh, core, x, z0 = tm >> 3, (tm >> 1) & 3, tm & 1, fiber >> 1, fiber & 1
    z2, z1 = zh >> 1, zh & 1
    late = z0 ^ z2
    first = 1 ^ z1 ^ late

    def send(part, perm, axes=AXES):
        return lax.ppermute(part, axes, perm)

    got = ([], [])
    for step in (0, 1):
        rows = lax.dynamic_slice_in_dim(waveform, 256 * (step ^ z2), 256, 0)
        part = rows.reshape(2, 128, 16, HOP)[:, 40:88]
        got[0].append(send(part, bulk_route(step)))
    up = [(i, i + 1) for i in range(7)]
    row_low = send(waveform[511:], up, "fiber")
    row_high = send(waveform[:1], [(j, i) for i, j in up], "fiber")
    wave, row_low, row_high = lax.optimization_barrier((waveform, row_low, row_high))
    sides = [row_low] + [wave[i : i + 1] for i in (128, 127, 256, 255, 384, 383)] + [row_high]
    sides = jnp.concatenate(sides, axis=0).reshape(4, 2, 16, HOP)
    for step in (0, 1):
        rows = lax.dynamic_slice_in_dim(wave, 256 * (step ^ z2), 256, 0)
        rows = rows.reshape(2, 128, 16, HOP)
        extra = lax.dynamic_slice_in_dim(sides, 2 * (step ^ z2), 2, 0)
        part = jnp.concatenate([rows[:, :40], rows[:, 88:], extra], axis=1)
        got[1].append(send(part, bulk_route(step)))

    taps = pl.pallas_call(
        flip_kernel,
        out_shape=jax.ShapeDtypeStruct((256, 512), jnp.bfloat16),
        cost_estimate=pl.CostEstimate(flops=0, bytes_accessed=1 << 19, transcendentals=0),
        name="flip",
    )(filters)

    keep = jnp.where((late == 0) & (((y - x + TURN) & 3) == 0), 0, 1)
    where = jnp.stack([first, core, keep]).astype(jnp.int32)
    recv = []
    for half in (0, 1):
        size = 82 if half else 48
        theirs = [lax.dynamic_index_in_dim(g, 1 - core, 0, False) for g in got[half]]
        other = send(jnp.stack(theirs), OTHER_CORE, "tm")
        feats = pl.pallas_call(
            filter_kernel,
            out_shape=jax.ShapeDtypeStruct((8, size // 2 + 2, GW, 128), jnp.bfloat16),
            in_specs=[SMEM] + [VMEM] * 4,
            out_specs=VMEM,
            scratch_shapes=[
                pltpu.VMEM((size, 96, HOP), jnp.bfloat16),
                pltpu.VMEM((256, 512), jnp.float32),
            ],
            cost_estimate=pl.CostEstimate(
                flops=size * 2 * 64 * 512 * 256, bytes_accessed=size * 49152, transcendentals=0
            ),
            name="filterbank",
        )(where, *got[half], other, taps)
        recv.append(lax.all_to_all(feats, "fiber", 0, 0, tiled=True))

    edge = jnp.array([-1], jnp.int32)
    sec = lax.dynamic_slice_in_dim(
        jnp.concatenate([edge, channel_section, edge]), tm * 128, 130, 0
    )
    middle = sec[1:-1]
    table = lax.dynamic_slice_in_dim(section_bank, fiber, 1, 1)
    onehot = (middle[:, None] == jnp.arange(table.shape[0], dtype=jnp.int32)[None, :]).astype(
        jnp.int32
    )
    choose = jnp.sum(onehot * table[:, 0][None, :], axis=1)
    flags = jnp.stack([choose, sec[:-2] == middle, sec[2:] == middle]).astype(jnp.int32)
    kern = conv_bank[:, 0].transpose(0, 3, 2, 1, 4).reshape(64, 288)
    weights = pl.pallas_call(
        weight_kernel,
        out_shape=jax.ShapeDtypeStruct((16, 256, 960), jnp.bfloat16),
        grid_spec=pltpu.PrefetchScalarGridSpec(
            num_scalar_prefetch=1,
            grid=(16,),
            in_specs=[whole(64, 288)],
            out_specs=pl.BlockSpec((1, 256, 960), lambda i, s: (i, 0, 0)),
            scratch_shapes=[pltpu.VMEM((8, 64, 960), jnp.float32)],
        ),
        cost_estimate=pl.CostEstimate(
            flops=8 * 2 * 64 * 288 * 960, bytes_accessed=8 << 20, transcendentals=0
        ),
        name="weights",
    )(flags, kern)

    q = jnp.arange(8, dtype=jnp.int32)
    slot = (2 * ((y + TURN - (q >> 1)) & 3) + ((q & 1) ^ z2)).astype(jnp.int32)
    at = jnp.arange(21 * 128, dtype=jnp.int32)
    source = jnp.where(at % 64 >= 61, (at % 128) // 64 * 64 + 3 * (at // 128) + at % 64 - 61, -1)
    spread = (jnp.arange(128, dtype=jnp.int32)[:, None] == source[None, :]).astype(jnp.bfloat16)
    late_rows = pltpu.VMEM((42, 8, GW, 128), jnp.bfloat16)
    part, side = pl.pallas_call(
        inner_kernel,
        out_shape=(
            jax.ShapeDtypeStruct((128, GW, 512), jnp.bfloat16),
            jax.ShapeDtypeStruct((3, 18, GW, 512), jnp.bfloat16),
        ),
        grid_spec=pltpu.PrefetchScalarGridSpec(
            num_scalar_prefetch=1,
            grid=(4,),
            in_specs=[
                whole(8, 26, GW, 128),
                whole(128, 21 * 128),
                pl.BlockSpec((1, 256, 960), lambda i, s: (i + 6, 0, 0)),
            ],
            out_specs=(
                pl.BlockSpec((8, GW, 512), lambda i, s: (i + 6, 0, 0)),
                whole(3, 18, GW, 512),
            ),
            scratch_shapes=[pltpu.VMEM((3, 48, GW, 512), jnp.bfloat16), late_rows],
        ),
        cost_estimate=pl.CostEstimate(
            flops=6 * 2 * 256 * 960 * 512, bytes_accessed=8 << 20, transcendentals=0
        ),
        name="conv_inner",
    )(slot, recv[0], spread, weights)
    return pl.pallas_call(
        outer_kernel,
        out_shape=jax.ShapeDtypeStruct((128, GW, 512), jnp.bfloat16),
        grid_spec=pltpu.PrefetchScalarGridSpec(
            num_scalar_prefetch=1,
            grid=(12,),
            in_specs=[
                whole(8, 43, GW, 128),
                whole(128, 21 * 128),
                whole(3, 18, GW, 512),
                pl.BlockSpec((1, 256, 960), lambda i, s: (i + 4 * (i // 6), 0, 0)),
                pl.BlockSpec(memory_space=pl.ANY),
            ],
            out_specs=pl.BlockSpec((8, GW, 512), lambda i, s: (i + 4 * (i // 6), 0, 0)),
            scratch_shapes=[pltpu.VMEM((3, 100, GW, 512), jnp.bfloat16), late_rows],
        ),
        input_output_aliases={5: 0},
        cost_estimate=pl.CostEstimate(
            flops=10 * 2 * 256 * 960 * 512, bytes_accessed=8 << 20, transcendentals=0
        ),
        name="conv_outer",
    )(slot, recv[1], spread, side, weights, part)


def solution(mesh):
    placed = (P("fiber", "tm"), P(), P(), P(), P(None, "fiber", None, None, None, None))

    return jax.shard_map(
        shards, mesh=mesh, in_specs=placed, out_specs=P("tm", "fiber", None), check_vma=False
    )
```
